128 devices in a mesh: dom: 32 (over y, x, core), rep: 4 (over z).
Axes of the slice: x: 4, y: 4, z: 4, core: 2. Of those that a mesh axis runs over, the one named last changes fastest.
Arguments:
- right_sides: float32 [4, 192, 16, 384], P(None, 'dom', 'rep'), may hold values from -6 to 6
- diag_inverse: bfloat16 [4, 192, 384, 384], P(None, 'dom'), may hold values from -0.3125 to 0.3125
- panel_mats: bfloat16 [3, 2048, 384, 384], P(None, ('dom', 'rep')), may hold values from -0.08984375 to 0.08984375
- panel_src: int32 [3, 2048], P(None, ('dom', 'rep')), may hold values from 0 to 17, as said below
- panel_dst: int32 [3, 2048], P(None, ('dom', 'rep')), may hold values from -1 to 191, as said below
Outputs:
- solution: float32 [4, 192, 16, 384], P(None, 'dom', 'rep')
The draws below stay inside these ranges and needn't reach their ends.
Inputs may be any that keep to these rules, and one draw needn't show every extreme that they name: `panel_src`: an entry of row l is below (l + 1) * 6, so the source tile lies in a level at most l; most of the entries lie in level l itself. A live entry of a list owned by dom index o names a tile of dom index (o + j) mod 32 with -2 <= j <= 2 or j = 16. Among the 16 entries of one device's list for one row, at most 3 live entries have the same destination dom index (panel_dst // 6), and in every list some dom index has exactly 3; lists of low dom indices tend to hold more live entries than those of high ones.
All inputs are finite; a program needn't handle non-finite values.
Results may differ from the reference program's by a relative error of at most 0.012.
Values may be sent and summed in bfloat16 or wider, within the bound.
No kernel may reach another device: no remote copies, remote signals or barrier semaphores. Data moves between devices by JAX's collectives and lax.ppermute only.
A program may use at most 128 MiB of HBM per device.

```python
import jax
import jax.numpy as jnp
from jax import lax

CELLS = 128
NRHS = 16
TPL = 6
LEVELS = 4
HALF = 2
PPR = 16
TILES = 192
PANELS = 2048
N_DOM = 32
N_REP = 4


def draw_panel_src(key, part):
    level_rows = LEVELS - 1
    entry_count = N_DOM * N_REP * PPR
    key_any, key_recent, key_choose = jax.random.split(jax.random.fold_in(key, 11), 3)
    row_index = jnp.arange(level_rows, dtype=jnp.int32)[:, None]
    anywhere = jax.random.randint(key_any, (level_rows, entry_count), 0, (row_index + 1) * TPL)
    recent = row_index * TPL + jax.random.randint(key_recent, (level_rows, entry_count), 0, TPL)
    chooser = jax.random.randint(key_choose, (level_rows, entry_count), 0, 2)
    return jnp.where(chooser == 0, recent, anywhere).astype(jnp.int32)


def draw_panel_dst(key, part):
    level_rows = LEVELS - 1
    block_count = N_DOM * N_REP
    hood = 2 * HALF + 2
    subkeys = jax.random.split(jax.random.fold_in(key, 23), 4)
    position = jnp.arange(PPR, dtype=jnp.int32)[None, None, :]
    owner = (jnp.arange(block_count, dtype=jnp.int32) // N_REP)[None, :, None]
    turn = jax.random.randint(subkeys[0], (level_rows, block_count, 1), 0, hood)
    klass = (position % hood + turn) % hood
    reach = jnp.where(klass == hood - 1, N_DOM // 2, klass - HALF)
    target = (owner + reach) % N_DOM
    dropper = jax.random.randint(subkeys[1], (level_rows, block_count, PPR), 0, 2 * N_DOM)
    padded = (position % hood != 0) & (dropper < owner + 1)
    column_slot = jax.random.randint(subkeys[2], (level_rows, block_count, PPR), 0, TPL)
    entries = jnp.where(padded, -1, target * TPL + column_slot)
    rotation = jax.random.randint(subkeys[3], (level_rows, block_count, 1), 0, PPR)
    reorder = (position + rotation) % PPR
    entries = jnp.take_along_axis(entries, reorder, axis=2)
    return entries.reshape(level_rows, block_count * PPR).astype(jnp.int32)


def block_levels(stream_key, extent, cuts, least, largest):
    gain, own = 1.0, jax.random.fold_in(stream_key, 6)
    for dim, blocks in cuts:
        heights = jnp.exp(jax.random.uniform(jax.random.fold_in(own, dim), (blocks,), jnp.float32, least / len(cuts), largest / len(cuts)))
        gain = gain * jnp.repeat(heights, extent[dim] // blocks).reshape([-1 if axis == dim else 1 for axis in range(len(extent))])
    return gain


def gaussian(key, extent, spread, limit, cuts=(), held_as=jnp.bfloat16):
    values = jax.random.normal(key, extent, jnp.float32) * spread
    if len(cuts) > 0:
        values = block_levels(key, extent, cuts, -0.22, 0.18) * values
    return jnp.clip(values, min=-limit, max=limit).astype(held_as)


def setup_inputs(seed: int = 0) -> dict:
    key_list = jax.random.split(jax.random.key(seed), 6)
    right_sides = gaussian(key_list[0], (LEVELS, TILES, NRHS, 3 * CELLS), 1.0, 6.0, ((1, 32), (2, 4)), jnp.float32)
    diag_inverse = gaussian(key_list[1], (LEVELS, TILES, 3 * CELLS, 3 * CELLS), (3 * CELLS) ** -0.5, 0.3125, ((1, 32),))
    panel_mats = gaussian(key_list[2], (LEVELS - 1, PANELS, 3 * CELLS, 3 * CELLS), 0.015, 0.08984375, ((1, 128),))
    panel_src = draw_panel_src(jax.random.fold_in(key_list[5], 71), 0)
    panel_dst = draw_panel_dst(jax.random.fold_in(key_list[5], 71), 0)
    return {"right_sides": right_sides, "diag_inverse": diag_inverse, "panel_mats": panel_mats, "panel_src": panel_src, "panel_dst": panel_dst}


def reference(right_sides, diag_inverse, panel_mats, panel_src, panel_dst):
    highest = lax.Precision.HIGHEST
    tile_total = N_DOM * TPL
    owner_dom = jnp.arange(N_DOM * N_REP * PPR, dtype=jnp.int32) // (N_REP * PPR)
    solved_all = []
    for level_index in range(LEVELS):
        residual = right_sides[level_index]
        if level_index > 0:
            history = jnp.stack([entry.astype(jnp.bfloat16) for entry in solved_all])
            source_ids = panel_src[level_index - 1]
            source_level = (source_ids // TPL).astype(jnp.int32)
            source_pos = (owner_dom * TPL + source_ids % TPL).astype(jnp.int32)
            sources = history[source_level, source_pos]
            contribution = jnp.einsum('qcx,qxy->qcy', sources.astype(jnp.float32), panel_mats[level_index - 1].astype(jnp.float32), precision=highest)
            onehot = (panel_dst[level_index - 1][:, None] == jnp.arange(tile_total, dtype=jnp.int32)[None, :]).astype(jnp.float32)
            incoming = jnp.einsum('qt,qcy->tcy', onehot, contribution, precision=highest)
            residual = residual - incoming
        rounded = lax.optimization_barrier(residual.astype(jnp.bfloat16))
        solved = jnp.einsum('tcx,txy->tcy', rounded.astype(jnp.float32), diag_inverse[level_index].astype(jnp.float32), precision=highest)
        solved_all.append(solved)
    return jnp.stack(solved_all)
```

```python
import functools

import jax
import jax.numpy as jnp
from jax import lax
from jax.experimental import pallas as pl
from jax.experimental.pallas import tpu as pltpu
from jax.sharding import PartitionSpec as P

HALF = 2
HOOD = 2 * HALF + 2


def passed_along(value, axis, by):
    size = lax.axis_size(axis)
    return lax.ppermute(value, axis, [(i, (i + by) % size) for i in range(size)])


def level_body(level, last, *refs):
    refs = list(refs)
    rep_ref = refs.pop(0)
    src_ref, slot_ref = (refs.pop(0), refs.pop(0)) if not last else (None, None)
    parts = [refs.pop(0) for _ in range(4)]
    diag_ref = refs.pop(0)
    mats_ref = refs.pop(0) if not last else None
    prev = [refs.pop(0) for _ in range(level)]
    out_ref = refs.pop(0)
    if last:
        (solved_scr,) = refs
    else:
        stored_ref = refs.pop(0)
        messages = [refs.pop(0) for _ in range(HOOD)]
        solved_scr, store_scr, acc_scr = refs
    tiles, cols, _ = parts[0].shape
    group = cols // 4
    for t in range(tiles):
        residual = sum(part[t].astype(jnp.float32) for part in parts).astype(jnp.bfloat16)
        solved = jnp.dot(residual, diag_ref[t], preferred_element_type=jnp.float32)
        solved_scr[t] = solved
        if not last:
            stored_ref[t] = solved.astype(jnp.bfloat16)
            store_scr[level * tiles + t] = solved.astype(jnp.bfloat16)
    own = solved_scr[:, :group, :]
    for other in range(1, cols // group):
        own = jnp.where(rep_ref[0] == other, solved_scr[:, other * group : (other + 1) * group, :], own)
    if last:
        for earlier in range(level):
            out_ref[earlier] = prev[earlier][...]
        out_ref[level] = own
        return
    out_ref[...] = own
    for earlier in range(level):
        for t in range(tiles):
            store_scr[earlier * tiles + t] = prev[earlier][t]
    acc_scr[...] = jnp.zeros_like(acc_scr)
    for p in range(mats_ref.shape[0]):
        update = jnp.dot(store_scr[src_ref[p]], mats_ref[p], preferred_element_type=jnp.float32)
        slot = slot_ref[p]
        acc_scr[slot] = acc_scr[slot] + update
    for j in range(HOOD):
        messages[j][...] = acc_scr[j * tiles : (j + 1) * tiles].astype(jnp.bfloat16)


def run_level(level, last, rep, ids, parts, diag, mats, prev, out_shape):
    tiles, cols, span = parts[0].shape
    group = cols // 4
    smem = pl.BlockSpec(memory_space=pltpu.SMEM)
    vmem = pl.BlockSpec(memory_space=pltpu.VMEM)
    args = [rep, *ids, *parts, diag]
    specs = [smem] * (1 + len(ids)) + [vmem] * 5
    if not last:
        args.append(mats)
        specs.append(vmem)
    args += prev
    specs += [vmem] * len(prev)
    scratch = [pltpu.VMEM((tiles, cols, span), jnp.float32)]
    if last:
        outs = jax.ShapeDtypeStruct(out_shape, jnp.float32)
        out_specs = vmem
    else:
        block = jax.ShapeDtypeStruct((tiles, cols, span), jnp.bfloat16)
        outs = [jax.ShapeDtypeStruct((tiles, group, span), jnp.float32), block] + [block] * HOOD
        out_specs = [vmem] * len(outs)
        scratch.append(pltpu.VMEM(((level + 1) * tiles, cols, span), jnp.bfloat16))
        scratch.append(pltpu.VMEM((HOOD * tiles + 1, cols, span), jnp.float32))
    return pl.pallas_call(
        functools.partial(level_body, level, last),
        out_shape=outs,
        in_specs=specs,
        out_specs=out_specs,
        scratch_shapes=scratch,
        compiler_params=pltpu.CompilerParams(vmem_limit_bytes=40 << 20),
    )(*args)


def per_device(right_sides, diag_inverse, panel_mats, panel_src, panel_dst):
    levels, tiles, group, span = right_sides.shape
    dom_size = lax.axis_size("dom")
    rep_size = lax.axis_size("rep")
    far = dom_size // 2
    rep = lax.axis_index("rep").astype(jnp.int32)
    owner = lax.axis_index("dom")
    cols = group * rep_size
    place = lax.broadcasted_iota(jnp.int32, (levels, tiles, cols, span), 2) // group == rep
    own_rhs = jnp.where(place, jnp.tile(right_sides, (1, 1, rep_size, 1)), 0.0)
    distance = (panel_dst // tiles - owner) % dom_size
    reach = jnp.where(distance == far, HOOD - 1, (distance + HALF) % dom_size)
    slots = jnp.where(panel_dst >= 0, reach * tiles + panel_dst % tiles, HOOD * tiles)
    partial = own_rhs[0].astype(jnp.bfloat16)
    store = []
    results = []
    for level in range(levels):
        parts = [partial] + [passed_along(partial, "rep", by) for by in range(1, rep_size)]
        if level + 1 == levels:
            return run_level(
                level, True, rep[None], [], parts, diag_inverse[level], None, results, right_sides.shape
            )
        solved, stored, *messages = run_level(
            level,
            False,
            rep[None],
            [panel_src[level], slots[level]],
            parts,
            diag_inverse[level],
            panel_mats[level],
            store,
            None,
        )
        results.append(solved)
        store.append(stored)
        incoming = jnp.zeros((tiles, cols, span), jnp.float32)
        for index in range(HOOD):
            offset = far if index == HOOD - 1 else index - HALF
            piece = messages[index]
            if offset != 0:
                piece = passed_along(piece, "dom", offset)
            incoming = incoming + piece.astype(jnp.float32)
        partial = (own_rhs[level + 1] - incoming).astype(jnp.bfloat16)


def solution(mesh):
    return jax.shard_map(
        per_device,
        mesh=mesh,
        in_specs=(
            P(None, "dom", "rep", None),
            P(None, "dom", None, None),
            P(None, ("dom", "rep"), None, None),
            P(None, ("dom", "rep")),
            P(None, ("dom", "rep")),
        ),
        out_specs=P(None, "dom", "rep", None),
        check_vma=False,
    )
```

```python
import functools

import jax
import jax.numpy as jnp
from jax import lax
from jax.experimental import pallas as pl
from jax.experimental.pallas import tpu as pltpu
from jax.sharding import PartitionSpec as P

HALF = 2
OWN, FAR, SIBLING, HANDED, PASSED, DIRECT = range(6)
GROUPS = 6
BACK = (2, 1, 3)
CHUNKS = 4


def dom_permute(value, target):
    size = lax.axis_size("dom")
    return lax.ppermute(value, "dom", [(i, target(i) % size) for i in range(size)])


def to_sibling(value):
    return dom_permute(value, lambda i: i ^ 1)


def to_far(value):
    half = lax.axis_size("dom") // 2
    return dom_permute(value, lambda i: i + half)


def to_next_chip(value):
    return dom_permute(value, lambda i: i + 2 if i % 2 else i - 2)


def along_rep(value, by):
    size = lax.axis_size("rep")
    return lax.ppermute(value, "rep", [(i, (i + by) % size) for i in range(size)])


def place_columns(parts, rep, group):
    size = len(parts)
    blocks = [part[...].astype(jnp.float32) for part in parts]
    placed = []
    for index in range(size):
        chosen = blocks[0]
        for block, back in zip(blocks[1:], BACK):
            chosen = jnp.where((rep + size - back) % size == index, block, chosen)
        placed.append(chosen)
    return placed


def level_body(level, last, *refs):
    refs = list(refs)
    take = lambda count: [refs.pop(0) for _ in range(count)]
    (rep_ref,) = take(1)
    ids_ref, rhs_hbm = take(2) if not last else (None, None)
    parts = take(4)
    (diag_ref,) = take(1)
    (mats_ref,) = take(1) if not last else (None,)
    prev = take(level)
    (out_ref,) = take(1)
    if not last:
        stored_ref, own_ref, far_ref, sibling_ref, chip_ref = take(5)
    (solved_scr,) = take(1)
    if not last:
        store_scr, acc_scr, rhs_ref, rhs_sem = take(4)
    tiles, cols, _ = solved_scr.shape
    group = cols // 4
    copies = []
    if not last:
        rhs_copy = pltpu.make_async_copy(rhs_hbm.at[level + 1], rhs_ref, rhs_sem.at[0])
    if level == 0:
        diag_hbm, mats_hbm = diag_ref, mats_ref
        diag_ref, mats_ref, sems = take(3)
        copies = [pltpu.make_async_copy(diag_hbm.at[0], diag_ref, sems.at[0])]
        for chunk in range(CHUNKS):
            some = pl.ds(chunk * (mats_ref.shape[0] // CHUNKS), mats_ref.shape[0] // CHUNKS)
            copies.append(pltpu.make_async_copy(mats_hbm.at[0, some], mats_ref.at[some], sems.at[1 + chunk]))
        for copy in copies:
            copy.start()
        rhs_copy.start()
        for index, block in enumerate(place_columns(parts, rep_ref[0], group)):
            solved_scr[:, index * group : (index + 1) * group, :] = block
        residuals = [solved_scr[t].astype(jnp.bfloat16) for t in range(tiles)]
        copies[0].wait()
    else:
        if not last:
            rhs_copy.start()
        residuals = [
            sum(part[t].astype(jnp.float32) for part in parts).astype(jnp.bfloat16) for t in range(tiles)
        ]
    for t in range(tiles):
        solved = jnp.dot(residuals[t], diag_ref[t], preferred_element_type=jnp.float32)
        solved_scr[t] = solved
        if not last:
            stored_ref[t] = solved.astype(jnp.bfloat16)
            store_scr[level * tiles + t] = solved.astype(jnp.bfloat16)
    own = solved_scr[:, :group, :]
    for other in range(1, cols // group):
        own = jnp.where(rep_ref[0] == other, solved_scr[:, other * group : (other + 1) * group, :], own)
    if last:
        for earlier in range(level):
            out_ref[earlier] = prev[earlier][...]
        out_ref[level] = own
        return
    out_ref[...] = own
    for earlier in range(level):
        for t in range(tiles):
            store_scr[earlier * tiles + t] = prev[earlier][t]
    acc_scr[...] = jnp.zeros_like(acc_scr)
    count = mats_ref.shape[0]
    for p in range(count):
        if copies and p % (count // CHUNKS) == 0:
            copies[1 + p // (count // CHUNKS)].wait()
        update = jnp.dot(store_scr[ids_ref[0, level, p]], mats_ref[p], preferred_element_type=jnp.float32)
        slot = ids_ref[1, level, p]
        acc_scr[slot] = acc_scr[slot] + update

    def sums(index):
        return acc_scr[index * tiles : (index + 1) * tiles]

    far_ref[...] = sums(FAR).astype(jnp.bfloat16)
    sibling_ref[0] = sums(HANDED).astype(jnp.bfloat16)
    sibling_ref[1] = sums(SIBLING).astype(jnp.bfloat16)
    chip_ref[0] = sums(PASSED).astype(jnp.bfloat16)
    chip_ref[1] = sums(DIRECT).astype(jnp.bfloat16)
    rhs_copy.wait()
    rhs = rhs_ref[...]
    for index in range(cols // group):
        rows = slice(index * group, (index + 1) * group)
        own_ref[:, rows, :] = jnp.where(rep_ref[0] == index, rhs, 0.0) - acc_scr[OWN * tiles : (OWN + 1) * tiles, rows, :]


def run_level(level, last, rep, ids, parts, diag, mats, prev, right_sides):
    levels, tiles, group, span = right_sides.shape
    cols = 4 * group
    smem = pl.BlockSpec(memory_space=pltpu.SMEM)
    vmem = pl.BlockSpec(memory_space=pltpu.VMEM)
    hbm = pl.BlockSpec(memory_space=pltpu.HBM)
    weights = hbm if level == 0 else vmem
    args = [rep]
    specs = [smem]
    if not last:
        args += [ids, right_sides]
        specs += [smem, hbm]
    args += [*parts, diag]
    specs += [vmem] * len(parts) + [weights]
    if not last:
        args.append(mats)
        specs.append(weights)
    args += prev
    specs += [vmem] * len(prev)
    scratch = [pltpu.VMEM((tiles, cols, span), jnp.float32)]
    if last:
        outs = jax.ShapeDtypeStruct(right_sides.shape, jnp.float32)
        out_specs = vmem
    else:
        block = jax.ShapeDtypeStruct((tiles, cols, span), jnp.bfloat16)
        pair = jax.ShapeDtypeStruct((2, tiles, cols, span), jnp.bfloat16)
        outs = [
            jax.ShapeDtypeStruct((tiles, group, span), jnp.float32),
            block,
            jax.ShapeDtypeStruct((tiles, cols, span), jnp.float32),
            block,
            pair,
            pair,
        ]
        out_specs = [vmem] * len(outs)
        scratch.append(pltpu.VMEM(((level + 1) * tiles, cols, span), jnp.bfloat16))
        scratch.append(pltpu.VMEM((GROUPS * tiles + 1, cols, span), jnp.float32))
        scratch.append(pltpu.VMEM((tiles, group, span), jnp.float32))
        scratch.append(pltpu.SemaphoreType.DMA((1,)))
    if level == 0:
        scratch.append(pltpu.VMEM(diag.shape[1:], diag.dtype))
        scratch.append(pltpu.VMEM(mats.shape[1:], mats.dtype))
        scratch.append(pltpu.SemaphoreType.DMA((1 + CHUNKS,)))
    return pl.pallas_call(
        functools.partial(level_body, level, last),
        out_shape=outs,
        in_specs=specs,
        out_specs=out_specs,
        scratch_shapes=scratch,
        compiler_params=pltpu.CompilerParams(vmem_limit_bytes=12 << 20),
    )(*args)


def fetch_body(level, with_mats, *refs):
    count = 1 + with_mats
    sems = refs[-1]
    copies = [
        pltpu.make_async_copy(refs[1 + i].at[level], refs[1 + count + i], sems.at[i]) for i in range(count)
    ]
    for copy in copies:
        copy.start()
    for copy in copies:
        copy.wait()


def fetch(level, after, *weights):
    vmem = pl.BlockSpec(memory_space=pltpu.VMEM)
    return pl.pallas_call(
        functools.partial(fetch_body, level, len(weights) - 1),
        out_shape=[pltpu.VMEM(w.shape[1:], w.dtype) for w in weights],
        in_specs=[vmem] + [pl.BlockSpec(memory_space=pltpu.HBM)] * len(weights),
        out_specs=[vmem] * len(weights),
        scratch_shapes=[pltpu.SemaphoreType.DMA((len(weights),))],
        compiler_params=pltpu.CompilerParams(vmem_limit_bytes=1 << 20),
    )(after, *weights)


def slots_of(panel_dst, tiles):
    dom_size = lax.axis_size("dom")
    owner = lax.axis_index("dom")
    distance = (panel_dst // tiles - owner) % dom_size
    near = (distance + HALF) % dom_size - HALF
    onward = jnp.where(owner % 2 == 1, near, -near)
    group = jnp.where(
        distance == dom_size // 2,
        FAR,
        jnp.where(
            onward == 0,
            OWN,
            jnp.where(
                onward == 1, PASSED, jnp.where(onward == 2, DIRECT, jnp.where(onward == -1, SIBLING, HANDED))
            ),
        ),
    )
    return jnp.where(panel_dst >= 0, group * tiles + panel_dst % tiles, GROUPS * tiles)


def per_device(right_sides, diag_inverse, panel_mats, panel_src, panel_dst):
    levels, tiles, group, span = right_sides.shape
    rep = lax.axis_index("rep").astype(jnp.int32)
    cols = group * lax.axis_size("rep")
    first = lax.broadcasted_iota(jnp.int32, (2, tiles, cols, span), 0) == 0
    ids = jnp.stack([panel_src, slots_of(panel_dst, tiles)])
    partial = right_sides[0].astype(jnp.bfloat16)
    diag_inverse, panel_mats, rhs = (
        pltpu.with_memory_space_constraint(x, pltpu.HBM) for x in (diag_inverse, panel_mats, right_sides)
    )
    diag, mats = diag_inverse, panel_mats
    store = []
    results = []
    for level in range(levels):
        last = level + 1 == levels
        parts = [partial] + [along_rep(partial, by) for by in BACK]
        if last:
            return run_level(level, last, rep[None], None, parts, diag, None, results, rhs)
        solved, stored, own, far, sibling, chip = run_level(
            level, last, rep[None], ids, parts, diag, mats, store, rhs
        )
        results.append(solved)
        store.append(stored)
        from_sibling = to_sibling(sibling)
        from_far = to_far(far)
        handed = jnp.where(first, from_sibling.astype(jnp.float32), 0.0)
        chip = (chip.astype(jnp.float32) + handed).astype(jnp.bfloat16)
        from_chip = to_next_chip(chip)
        if level + 2 == levels:
            (diag,) = fetch(level + 1, chip, diag_inverse)
        else:
            diag, mats = fetch(level + 1, chip, diag_inverse, panel_mats)
        across = to_sibling(from_chip[0])
        incoming = sum(
            piece.astype(jnp.float32) for piece in (from_sibling[1], from_far, from_chip[1], across)
        )
        partial = (own - incoming).astype(jnp.bfloat16)


def solution(mesh):
    return jax.shard_map(
        per_device,
        mesh=mesh,
        in_specs=(
            P(None, "dom", "rep", None),
            P(None, "dom", None, None),
            P(None, ("dom", "rep"), None, None),
            P(None, ("dom", "rep")),
            P(None, ("dom", "rep")),
        ),
        out_specs=P(None, "dom", "rep", None),
        check_vma=False,
    )
```

```python
import functools

import jax
import jax.numpy as jnp
from jax import lax
from jax.experimental import pallas as pl
from jax.experimental.pallas import tpu as pltpu
from jax.sharding import PartitionSpec as P

HALF = 2
OWN, FAR, SIBLING, HANDED, PASSED, DIRECT = range(6)
GROUPS = 6
BACK = (2, 1, 3)
CHUNKS = 4


def dom_permute(value, target, sends=lambda i: True):
    size = lax.axis_size("dom")
    return lax.ppermute(value, "dom", [(i, target(i) % size) for i in range(size) if sends(i)])


def to_sibling(value):
    return dom_permute(value, lambda i: i ^ 1)


def to_far(value):
    half = lax.axis_size("dom") // 2
    return dom_permute(value, lambda i: i + half, lambda i: i % 2 == (i // 2 % 4 < 2))


def to_next_chip(value):
    return dom_permute(value, lambda i: i + 2 if i % 2 else i - 2)


def along_rep(value, by):
    size = lax.axis_size("rep")
    return lax.ppermute(value, "rep", [(i, (i + by) % size) for i in range(size)])


def place_columns(parts, rep):
    size = len(parts)
    blocks = [part[...].astype(jnp.float32) for part in parts]
    placed = []
    for index in range(size):
        chosen = blocks[0]
        for block, back in zip(blocks[1:], BACK):
            chosen = jnp.where((rep + size - back) % size == index, block, chosen)
        placed.append(chosen)
    return placed


def weight_copies(level, sources, targets, sems):
    copies = []
    for source, target in zip(sources, targets):
        step = target.shape[0] // 2 if target.shape[0] < 8 else target.shape[0] // CHUNKS
        for start in range(0, target.shape[0], step):
            some = pl.ds(start, step)
            copies.append(
                pltpu.make_async_copy(source.at[level, some], target.at[some], sems.at[len(copies)])
            )
    return copies


def level_body(level, last, ahead, *refs):
    refs = list(refs)
    take = lambda count: [refs.pop(0) for _ in range(count)]
    (rep_ref,) = take(1)
    (ids_ref,) = take(1) if not last else (None,)
    parts = take(4)
    (diag_ref,) = take(1)
    (mats_ref,) = take(1) if not last else (None,)
    prev = take(level)
    sources = take(ahead)
    (out_ref,) = take(1)
    if not last:
        stored_ref, own_ref, sibling_ref, far_ref, chip_ref = take(5)
    targets = take(ahead)
    (solved_scr,) = take(1)
    if not last:
        store_scr, acc_scr = take(2)
    copies = weight_copies(level + 1, sources, targets, take(1)[0]) if ahead else []
    for copy in copies:
        copy.start()
    tiles, cols, _ = solved_scr.shape
    group = cols // 4
    if level == 0:
        for index, block in enumerate(place_columns(parts, rep_ref[0])):
            solved_scr[:, index * group : (index + 1) * group, :] = block
        residuals = [solved_scr[t].astype(jnp.bfloat16) for t in range(tiles)]
    else:
        residuals = [
            sum(part[t].astype(jnp.float32) for part in parts).astype(jnp.bfloat16) for t in range(tiles)
        ]
    for t in range(tiles):
        solved = jnp.dot(residuals[t], diag_ref[t], preferred_element_type=jnp.float32)
        solved_scr[t] = solved
        if not last:
            stored_ref[t] = solved.astype(jnp.bfloat16)
            store_scr[level * tiles + t] = solved.astype(jnp.bfloat16)
    own = solved_scr[:, :group, :]
    for other in range(1, cols // group):
        own = jnp.where(rep_ref[0] == other, solved_scr[:, other * group : (other + 1) * group, :], own)
    if last:
        for earlier in range(level):
            out_ref[earlier] = prev[earlier][...]
        out_ref[level] = own
        return
    out_ref[...] = own
    for earlier in range(level):
        for t in range(tiles):
            store_scr[earlier * tiles + t] = prev[earlier][t]
    acc_scr[...] = jnp.zeros_like(acc_scr)
    for p in range(mats_ref.shape[0]):
        update = jnp.dot(
            store_scr[ids_ref[0, level, p]], mats_ref[p], preferred_element_type=jnp.float32
        )
        slot = ids_ref[1, level, p]
        acc_scr[slot] = acc_scr[slot] + update

    def sums(index):
        return acc_scr[index * tiles : (index + 1) * tiles].astype(jnp.bfloat16)

    own_ref[...] = sums(OWN)
    far_ref[0] = sums(FAR)
    far_ref[1] = sums(FAR)
    sibling_ref[0] = sums(HANDED)
    sibling_ref[1] = sums(SIBLING)
    sibling_ref[2] = sums(FAR)
    chip_ref[0] = sums(PASSED)
    chip_ref[1] = sums(DIRECT)
    for copy in copies:
        copy.wait()


def run_level(level, last, rep, ids, parts, weights, prev, ahead, shape):
    levels, tiles, group, span = shape
    cols = 4 * group
    smem = pl.BlockSpec(memory_space=pltpu.SMEM)
    vmem = pl.BlockSpec(memory_space=pltpu.VMEM)
    hbm = pl.BlockSpec(memory_space=pltpu.HBM)
    args = [rep]
    specs = [smem]
    if not last:
        args.append(ids)
        specs.append(smem)
    inner = [*parts, *weights, *prev]
    args += inner + ahead
    specs += [vmem] * len(inner) + [hbm] * len(ahead)
    scratch = [pltpu.VMEM((tiles, cols, span), jnp.float32)]
    if last:
        outs = jax.ShapeDtypeStruct(shape, jnp.float32)
        out_specs = vmem
    else:
        outs = [jax.ShapeDtypeStruct((tiles, group, span), jnp.float32)] + [
            jax.ShapeDtypeStruct((*lead, tiles, cols, span), jnp.bfloat16) for lead in ((), (), (3,), (2,), (2,))
        ]
        outs += [pltpu.VMEM(w.shape[1:], w.dtype) for w in ahead]
        out_specs = [vmem] * len(outs)
        scratch.append(pltpu.VMEM(((level + 1) * tiles, cols, span), jnp.bfloat16))
        scratch.append(pltpu.VMEM((GROUPS * tiles + 1, cols, span), jnp.float32))
        scratch.append(pltpu.SemaphoreType.DMA((2 + CHUNKS,)))
    return pl.pallas_call(
        functools.partial(level_body, level, last, len(ahead)),
        out_shape=outs,
        in_specs=specs,
        out_specs=out_specs,
        scratch_shapes=scratch,
        compiler_params=pltpu.CompilerParams(vmem_limit_bytes=6 << 20),
    )(*args)


def fetch_body(*refs):
    _, diag_hbm, mats_hbm, diag_ref, mats_ref, sems = refs
    copies = weight_copies(0, [diag_hbm, mats_hbm], [diag_ref, mats_ref], sems)
    for copy in copies:
        copy.start()
    for copy in copies:
        copy.wait()


def fetch(after, diag, mats):
    vmem = pl.BlockSpec(memory_space=pltpu.VMEM)
    hbm = pl.BlockSpec(memory_space=pltpu.HBM)
    return pl.pallas_call(
        fetch_body,
        out_shape=[pltpu.VMEM(w.shape[1:], w.dtype) for w in (diag, mats)],
        in_specs=[vmem, hbm, hbm],
        out_specs=[vmem, vmem],
        scratch_shapes=[pltpu.SemaphoreType.DMA((2 + CHUNKS,))],
        compiler_params=pltpu.CompilerParams(vmem_limit_bytes=1 << 20),
    )(after, diag, mats)


def slots_of(panel_dst, tiles):
    dom_size = lax.axis_size("dom")
    owner = lax.axis_index("dom")
    distance = (panel_dst // tiles - owner) % dom_size
    near = (distance + HALF) % dom_size - HALF
    onward = jnp.where(owner % 2 == 1, near, -near)
    group = jnp.where(
        distance == dom_size // 2,
        FAR,
        jnp.where(
            onward == 0,
            OWN,
            jnp.where(
                onward == 1, PASSED, jnp.where(onward == 2, DIRECT, jnp.where(onward == -1, SIBLING, HANDED))
            ),
        ),
    )
    return jnp.where(panel_dst >= 0, group * tiles + panel_dst % tiles, GROUPS * tiles)


def per_device(right_sides, diag_inverse, panel_mats, panel_src, panel_dst):
    levels, tiles, group, span = right_sides.shape
    rep_size = lax.axis_size("rep")
    rep = lax.axis_index("rep").astype(jnp.int32)
    cols = group * rep_size
    first = lax.broadcasted_iota(jnp.int32, (2, tiles, cols, span), 0) == 0
    ids = jnp.stack([panel_src, slots_of(panel_dst, tiles)])
    partial = right_sides[0].astype(jnp.bfloat16)
    place = lax.broadcasted_iota(jnp.int32, (levels, tiles, cols, span), 2) // group == rep
    own_rhs = jnp.where(place, jnp.concatenate([right_sides] * rep_size, 2), 0.0)
    diag_inverse, panel_mats = (
        pltpu.with_memory_space_constraint(x, pltpu.HBM) for x in (diag_inverse, panel_mats)
    )
    weights = fetch(partial, diag_inverse, panel_mats)
    store = []
    results = []
    for level in range(levels):
        last = level + 1 == levels
        parts = [partial] + [along_rep(partial, by) for by in BACK]
        ahead = [] if last else [diag_inverse] if level + 2 == levels else [diag_inverse, panel_mats]
        if last:
            return run_level(
                level, last, rep[None], None, parts, weights, results, ahead, right_sides.shape
            )
        solved, stored, own, sibling, far, chip, *weights = run_level(
            level, last, rep[None], ids, parts, weights, store, ahead, right_sides.shape
        )
        results.append(solved)
        store.append(stored)
        from_sibling = to_sibling(sibling)
        handed = jnp.where(first, from_sibling[:2].astype(jnp.float32), 0.0)
        from_far = to_far(jnp.where(first, far, from_sibling[1:]))
        from_chip = to_next_chip((chip.astype(jnp.float32) + handed).astype(jnp.bfloat16))
        across = to_sibling(
            (from_chip[0].astype(jnp.float32) + from_far[1].astype(jnp.float32)).astype(jnp.bfloat16)
        )
        incoming = sum(
            piece.astype(jnp.float32) for piece in (own, from_sibling[1], from_chip[1], from_far[0], across)
        )
        partial = (own_rhs[level + 1] - incoming).astype(jnp.bfloat16)


def solution(mesh):
    return jax.shard_map(
        per_device,
        mesh=mesh,
        in_specs=(
            P(None, "dom", "rep", None),
            P(None, "dom", None, None),
            P(None, ("dom", "rep"), None, None),
            P(None, ("dom", "rep")),
            P(None, ("dom", "rep")),
        ),
        out_specs=P(None, "dom", "rep", None),
        check_vma=False,
    )
```

```python
import functools

import jax
import jax.numpy as jnp
from jax import lax
from jax.experimental import pallas as pl
from jax.experimental.pallas import tpu as pltpu
from jax.sharding import PartitionSpec as P

HALF = 2
OWN, FAR, SIBLING, HANDED, PASSED, DIRECT = range(6)
GROUPS = 6
APART = (3, 2, 1)
CHUNKS = 4


def dom_permute(value, target):
    size = lax.axis_size("dom")
    return lax.ppermute(value, "dom", [(i, target(i) % size) for i in range(size)])


def to_sibling(value):
    return dom_permute(value, lambda i: i ^ 1)


def to_far(value):
    half = lax.axis_size("dom") // 2
    return dom_permute(value, lambda i: i + half)


def to_next_chip(value):
    return dom_permute(value, lambda i: i + 2 if i % 2 else i - 2)


def along_rep(value, apart):
    return lax.ppermute(value, "rep", [(i, i ^ apart) for i in range(lax.axis_size("rep"))])


def place_columns(parts, rep):
    size = len(parts)
    blocks = [part[...].astype(jnp.float32) for part in parts]
    placed = []
    for index in range(size):
        chosen = blocks[0]
        for block, apart in zip(blocks[1:], APART):
            chosen = jnp.where(rep == index ^ apart, block, chosen)
        placed.append(chosen)
    return placed


def level_body(level, last, *refs):
    refs = list(refs)
    take = lambda count: [refs.pop(0) for _ in range(count)]
    (rep_ref,) = take(1)
    (ids_ref,) = take(1) if not last else (None,)
    parts = take(4)
    (diag_ref,) = take(1)
    (mats_ref,) = take(1) if not last else (None,)
    prev = take(level)
    (out_ref,) = take(1)
    if not last:
        stored_ref, own_ref, sibling_ref, handed_ref, far_ref, chip_ref = take(6)
    (solved_scr,) = take(1)
    if not last:
        store_scr, acc_scr = take(2)
    tiles, cols, _ = solved_scr.shape
    group = cols // 4
    if level == 0:
        for index, block in enumerate(place_columns(parts, rep_ref[0])):
            solved_scr[:, index * group : (index + 1) * group, :] = block
        residuals = [solved_scr[t].astype(jnp.bfloat16) for t in range(tiles)]
    else:
        residuals = [
            sum(part[t].astype(jnp.float32) for part in parts).astype(jnp.bfloat16) for t in range(tiles)
        ]
    for t in range(tiles):
        solved = jnp.dot(residuals[t], diag_ref[level, t], preferred_element_type=jnp.float32)
        solved_scr[t] = solved
        if not last:
            stored_ref[t] = solved.astype(jnp.bfloat16)
            store_scr[level * tiles + t] = solved.astype(jnp.bfloat16)
    own = solved_scr[:, :group, :]
    for other in range(1, cols // group):
        own = jnp.where(rep_ref[0] == other, solved_scr[:, other * group : (other + 1) * group, :], own)
    if last:
        for earlier in range(level):
            out_ref[earlier] = prev[earlier][...]
        out_ref[level] = own
        return
    out_ref[...] = own
    for earlier in range(level):
        for t in range(tiles):
            store_scr[earlier * tiles + t] = prev[earlier][t]
    acc_scr[...] = jnp.zeros_like(acc_scr)
    for p in range(mats_ref.shape[1]):
        update = jnp.dot(
            store_scr[ids_ref[0, level, p]], mats_ref[level, p], preferred_element_type=jnp.float32
        )
        slot = ids_ref[1, level, p]
        acc_scr[slot] = acc_scr[slot] + update

    def sums(index):
        return acc_scr[index * tiles : (index + 1) * tiles].astype(jnp.bfloat16)

    own_ref[...] = sums(OWN)
    sibling_ref[...] = sums(SIBLING)
    handed_ref[...] = sums(HANDED)
    far_ref[...] = sums(FAR)
    chip_ref[0] = sums(PASSED)
    chip_ref[1] = sums(DIRECT)


def run_level(level, last, rep, ids, parts, weights, prev, shape):
    levels, tiles, group, span = shape
    cols = 4 * group
    smem = pl.BlockSpec(memory_space=pltpu.SMEM)
    vmem = pl.BlockSpec(memory_space=pltpu.VMEM)
    args = [rep]
    specs = [smem]
    if not last:
        args.append(ids)
        specs.append(smem)
    inner = [*parts, *weights, *prev]
    args += inner
    specs += [vmem] * len(inner)
    scratch = [pltpu.VMEM((tiles, cols, span), jnp.float32)]
    if last:
        outs = jax.ShapeDtypeStruct(shape, jnp.float32)
        out_specs = vmem
    else:
        outs = [jax.ShapeDtypeStruct((tiles, group, span), jnp.float32)] + [
            jax.ShapeDtypeStruct((*lead, tiles, cols, span), jnp.bfloat16) for lead in ((), (), (), (), (), (2,))
        ]
        out_specs = [vmem] * len(outs)
        scratch.append(pltpu.VMEM(((level + 1) * tiles, cols, span), jnp.bfloat16))
        scratch.append(pltpu.VMEM((GROUPS * tiles + 1, cols, span), jnp.float32))
    return pl.pallas_call(
        functools.partial(level_body, level, last),
        out_shape=outs,
        in_specs=specs,
        out_specs=out_specs,
        scratch_shapes=scratch,
        compiler_params=pltpu.CompilerParams(vmem_limit_bytes=6 << 20),
    )(*args)


def slots_of(panel_dst, owner, dom_size, tiles):
    target = jnp.zeros_like(panel_dst)
    for other in range(1, dom_size):
        target = target + (panel_dst >= other * tiles).astype(jnp.int32)
    distance = target - owner
    distance = jnp.where(distance < 0, distance + dom_size, distance)
    near = jnp.where(distance > dom_size // 2, distance - dom_size, distance)
    onward = jnp.where(owner % 2 == 1, near, -near)
    group = jnp.where(
        distance == dom_size // 2,
        FAR,
        jnp.where(
            onward == 0,
            OWN,
            jnp.where(
                onward == 1, PASSED, jnp.where(onward == 2, DIRECT, jnp.where(onward == -1, SIBLING, HANDED))
            ),
        ),
    )
    return jnp.where(panel_dst >= 0, group * tiles + panel_dst - target * tiles, GROUPS * tiles)


def fetch_body(dom_size, *refs):
    owner_ref, _, src_ref, dst_ref, diag_hbm, mats_hbm, ids_ref, diag_ref, mats_ref, sems = refs
    copies = [pltpu.make_async_copy(diag_hbm.at[pl.ds(0, 1)], diag_ref.at[pl.ds(0, 1)], sems.at[0])]
    step = mats_ref.shape[1] // CHUNKS
    for chunk in range(CHUNKS):
        some = pl.ds(chunk * step, step)
        copies.append(
            pltpu.make_async_copy(mats_hbm.at[pl.ds(0, 1), some], mats_ref.at[:, some], sems.at[1 + chunk])
        )
    copies.append(
        pltpu.make_async_copy(diag_hbm.at[pl.ds(1, 1)], diag_ref.at[pl.ds(1, 1)], sems.at[1 + CHUNKS])
    )
    for copy in copies:
        copy.start()
    ids_ref[0] = src_ref[...]
    ids_ref[1] = slots_of(dst_ref[...], owner_ref[0], dom_size, diag_ref.shape[1])
    for copy in copies:
        copy.wait()


def fetch(after, src, dst, diag, mats):
    vmem = pl.BlockSpec(memory_space=pltpu.VMEM)
    hbm = pl.BlockSpec(memory_space=pltpu.HBM)
    owner = lax.axis_index("dom").astype(jnp.int32)
    return pl.pallas_call(
        functools.partial(fetch_body, lax.axis_size("dom")),
        out_shape=[
            jax.ShapeDtypeStruct((2, *src.shape), jnp.int32),
            pltpu.VMEM((2, *diag.shape[1:]), diag.dtype),
            pltpu.VMEM((1, *mats.shape[1:]), mats.dtype),
        ],
        in_specs=[pl.BlockSpec(memory_space=pltpu.SMEM), vmem, vmem, vmem, hbm, hbm],
        out_specs=[vmem, vmem, vmem],
        scratch_shapes=[pltpu.SemaphoreType.DMA((2 + CHUNKS,))],
        compiler_params=pltpu.CompilerParams(vmem_limit_bytes=1 << 20),
    )(owner[None], after, src, dst, diag, mats)


def per_device(right_sides, diag_inverse, panel_mats, panel_src, panel_dst):
    levels, tiles, group, span = right_sides.shape
    rep_size = lax.axis_size("rep")
    rep = lax.axis_index("rep").astype(jnp.int32)
    cols = group * rep_size
    top = lax.broadcasted_iota(jnp.int32, (2, tiles, cols, span), 0) == 0
    partial = right_sides[0].astype(jnp.bfloat16)
    place = lax.broadcasted_iota(jnp.int32, (levels, tiles, cols, span), 2) // group == rep
    own_rhs = jnp.where(place, jnp.concatenate([right_sides] * rep_size, 2), 0.0)
    ids, early_diag, early_mats = fetch(
        partial,
        panel_src,
        panel_dst,
        *(pltpu.with_memory_space_constraint(x, pltpu.HBM) for x in (diag_inverse, panel_mats)),
    )
    late_diag, late_mats = (
        pltpu.with_memory_space_constraint(x, pltpu.VMEM) for x in (diag_inverse, panel_mats)
    )
    store = []
    results = []
    for level in range(levels):
        last = level + 1 == levels
        parts = [partial] + [along_rep(partial, apart) for apart in APART]
        weights = [early_diag if level < 2 else late_diag, early_mats if level < 1 else late_mats]
        if last:
            return run_level(
                level, last, rep[None], None, parts, weights[:1], results, right_sides.shape
            )
        solved, stored, own, sibling, handed, far, chip = run_level(
            level, last, rep[None], ids, parts, weights, store, right_sides.shape
        )
        results.append(solved)
        store.append(stored)
        handed = jnp.where(top, to_sibling(handed), jnp.zeros_like(handed))
        from_chip = to_next_chip(
            (chip.astype(jnp.float32) + handed.astype(jnp.float32)).astype(jnp.bfloat16)
        )
        from_far = to_far(far)
        across = to_sibling(
            (from_chip[0].astype(jnp.float32) + sibling.astype(jnp.float32)).astype(jnp.bfloat16)
        )
        incoming = sum(piece.astype(jnp.float32) for piece in (own, from_chip[1], from_far, across))
        partial = (own_rhs[level + 1] - incoming).astype(jnp.bfloat16)


def solution(mesh):
    return jax.shard_map(
        per_device,
        mesh=mesh,
        in_specs=(
            P(None, "dom", "rep", None),
            P(None, "dom", None, None),
            P(None, ("dom", "rep"), None, None),
            P(None, ("dom", "rep")),
            P(None, ("dom", "rep")),
        ),
        out_specs=P(None, "dom", "rep", None),
        check_vma=False,
    )
```

```python
import functools

import jax
import jax.numpy as jnp
from jax import lax
from jax.experimental import pallas as pl
from jax.experimental.pallas import tpu as pltpu
from jax.sharding import PartitionSpec as P

HALF = 2
OWN, FAR, SIBLING, HANDED, PASSED, DIRECT = range(6)
GROUPS = 6
APART = (2, 3, 1)
CHUNKS = 4
SLOTS = 3


def dom_permute(value, target):
    size = lax.axis_size("dom")
    return lax.ppermute(value, "dom", [(i, target(i) % size) for i in range(size)])


def to_sibling(value):
    return dom_permute(value, lambda i: i ^ 1)


def to_far(value):
    half = lax.axis_size("dom") // 2
    return dom_permute(value, lambda i: i + half)


def to_next_chip(value):
    return dom_permute(value, lambda i: i + 2 if i % 2 else i - 2)


def along_rep(value, apart):
    return lax.ppermute(value, "rep", [(i, i ^ apart) for i in range(lax.axis_size("rep"))])


def place_columns(parts, rep):
    size = len(parts)
    blocks = [part[...].astype(jnp.float32) for part in parts]
    placed = []
    for index in range(size):
        chosen = blocks[0]
        for block, apart in zip(blocks[1:], APART):
            chosen = jnp.where(rep == index ^ apart, block, chosen)
        placed.append(chosen)
    return placed


def solve_body(level, last, *refs):
    refs = list(refs)
    take = lambda count: [refs.pop(0) for _ in range(count)]
    (rep_ref,) = take(1)
    (ids_ref,) = take(1) if not last else (None,)
    parts = take(4)
    (diag_ref,) = take(1)
    (mats_ref,) = take(1) if not last else (None,)
    prev = take(level)
    (out_ref,) = take(1)
    if not last:
        stored_ref, handed_ref = take(2)
    (solved_scr,) = take(1)
    if not last:
        store_scr, acc_scr, chosen_ref = take(3)
    tiles, cols, _ = solved_scr.shape
    group = cols // 4
    if level == 0:
        for index, block in enumerate(place_columns(parts, rep_ref[0])):
            solved_scr[:, index * group : (index + 1) * group, :] = block
        residuals = [solved_scr[t].astype(jnp.bfloat16) for t in range(tiles)]
    else:
        residuals = [
            sum(part[t].astype(jnp.float32) for part in parts).astype(jnp.bfloat16) for t in range(tiles)
        ]
    for t in range(tiles):
        solved = jnp.dot(residuals[t], diag_ref[level, t], preferred_element_type=jnp.float32)
        solved_scr[t] = solved
        if not last:
            stored_ref[t] = solved.astype(jnp.bfloat16)
            store_scr[level * tiles + t] = solved.astype(jnp.bfloat16)
    own = solved_scr[:, :group, :]
    for other in range(1, cols // group):
        own = jnp.where(rep_ref[0] == other, solved_scr[:, other * group : (other + 1) * group, :], own)
    if last:
        for earlier in range(level):
            out_ref[earlier] = prev[earlier][...]
        out_ref[level] = own
        return
    out_ref[...] = own
    for earlier in range(level):
        for t in range(tiles):
            store_scr[earlier * tiles + t] = prev[earlier][t]
    for r in range(SLOTS):
        chosen_ref[r] = 0
    count = jnp.int32(0)
    for p in range(mats_ref.shape[1]):
        row = ids_ref[1, level, p] - HANDED * tiles
        live = jnp.logical_and(row >= 0, row < tiles)
        chosen_ref[jnp.minimum(count, SLOTS)] = jnp.int32(p)
        count = count + live.astype(jnp.int32)
    acc_scr[...] = jnp.zeros_like(acc_scr)
    for r in range(SLOTS):
        p = chosen_ref[r]
        update = jnp.dot(
            store_scr[ids_ref[0, level, p]], mats_ref[level, p], preferred_element_type=jnp.float32
        )
        row = jnp.where(r < count, ids_ref[1, level, p] - HANDED * tiles, tiles)
        acc_scr[row] = acc_scr[row] + update
    handed_ref[...] = acc_scr[:tiles].astype(jnp.bfloat16)


def panels_body(level, *refs):
    refs = list(refs)
    take = lambda count: [refs.pop(0) for _ in range(count)]
    ids_ref, mats_ref = take(2)
    stores = take(level + 1)
    own_ref, sibling_ref, far_ref, chip_ref, store_scr, acc_scr = refs
    tiles = own_ref.shape[0]
    for earlier in range(level + 1):
        for t in range(tiles):
            store_scr[earlier * tiles + t] = stores[earlier][t]
    acc_scr[...] = jnp.zeros_like(acc_scr)
    for p in range(mats_ref.shape[1]):
        update = jnp.dot(
            store_scr[ids_ref[0, level, p]], mats_ref[level, p], preferred_element_type=jnp.float32
        )
        slot = ids_ref[1, level, p]
        acc_scr[slot] = acc_scr[slot] + update

    def sums(index):
        return acc_scr[index * tiles : (index + 1) * tiles].astype(jnp.bfloat16)

    own_ref[...] = sums(OWN)
    sibling_ref[...] = sums(SIBLING)
    far_ref[...] = sums(FAR)
    chip_ref[0] = sums(PASSED)
    chip_ref[1] = sums(DIRECT)


def run_solve(level, last, rep, ids, parts, weights, prev, shape):
    levels, tiles, group, span = shape
    cols = 4 * group
    smem = pl.BlockSpec(memory_space=pltpu.SMEM)
    vmem = pl.BlockSpec(memory_space=pltpu.VMEM)
    scalars = [rep] if last else [rep, ids]
    inner = [*parts, *weights, *prev]
    scratch = [pltpu.VMEM((tiles, cols, span), jnp.float32)]
    if last:
        outs = jax.ShapeDtypeStruct(shape, jnp.float32)
        out_specs = vmem
    else:
        block = jax.ShapeDtypeStruct((tiles, cols, span), jnp.bfloat16)
        outs = [jax.ShapeDtypeStruct((tiles, group, span), jnp.float32), block, block]
        out_specs = [vmem] * len(outs)
        scratch.append(pltpu.VMEM(((level + 1) * tiles, cols, span), jnp.bfloat16))
        scratch.append(pltpu.VMEM((tiles + 1, cols, span), jnp.float32))
        scratch.append(pltpu.SMEM((SLOTS + 1,), jnp.int32))
    return pl.pallas_call(
        functools.partial(solve_body, level, last),
        out_shape=outs,
        in_specs=[smem] * len(scalars) + [vmem] * len(inner),
        out_specs=out_specs,
        scratch_shapes=scratch,
        compiler_params=pltpu.CompilerParams(vmem_limit_bytes=6 << 20),
    )(*scalars, *inner)


def run_panels(level, ids, mats, stores):
    smem = pl.BlockSpec(memory_space=pltpu.SMEM)
    vmem = pl.BlockSpec(memory_space=pltpu.VMEM)
    tiles, cols, span = stores[0].shape
    return pl.pallas_call(
        functools.partial(panels_body, level),
        out_shape=[
            jax.ShapeDtypeStruct((*lead, tiles, cols, span), jnp.bfloat16) for lead in ((), (), (), (2,))
        ],
        in_specs=[smem] + [vmem] * (1 + len(stores)),
        out_specs=[vmem] * 4,
        scratch_shapes=[
            pltpu.VMEM(((level + 1) * tiles, cols, span), jnp.bfloat16),
            pltpu.VMEM((GROUPS * tiles + 1, cols, span), jnp.float32),
        ],
        compiler_params=pltpu.CompilerParams(vmem_limit_bytes=6 << 20),
    )(ids, mats, *stores)


def slots_of(panel_dst, owner, dom_size, tiles):
    target = jnp.zeros_like(panel_dst)
    for other in range(1, dom_size):
        target = target + (panel_dst >= other * tiles).astype(jnp.int32)
    distance = target - owner
    distance = jnp.where(distance < 0, distance + dom_size, distance)
    near = jnp.where(distance > dom_size // 2, distance - dom_size, distance)
    onward = jnp.where(owner % 2 == 1, near, -near)
    group = jnp.where(
        distance == dom_size // 2,
        FAR,
        jnp.where(
            onward == 0,
            OWN,
            jnp.where(
                onward == 1, PASSED, jnp.where(onward == 2, DIRECT, jnp.where(onward == -1, SIBLING, HANDED))
            ),
        ),
    )
    return jnp.where(panel_dst >= 0, group * tiles + panel_dst - target * tiles, GROUPS * tiles)


def fetch_body(dom_size, *refs):
    owner_ref, _, src_hbm, dst_hbm, diag_hbm, mats_hbm, ids_ref, diag_ref, mats_ref, dst_ref, sems = refs
    lists = [
        pltpu.make_async_copy(src_hbm, ids_ref.at[0], sems.at[2 + CHUNKS]),
        pltpu.make_async_copy(dst_hbm, dst_ref, sems.at[3 + CHUNKS]),
    ]
    for copy in lists:
        copy.start()
    copies = [pltpu.make_async_copy(diag_hbm.at[pl.ds(0, 1)], diag_ref.at[pl.ds(0, 1)], sems.at[0])]
    step = mats_ref.shape[1] // CHUNKS
    for chunk in range(CHUNKS):
        some = pl.ds(chunk * step, step)
        copies.append(
            pltpu.make_async_copy(mats_hbm.at[pl.ds(0, 1), some], mats_ref.at[:, some], sems.at[1 + chunk])
        )
    copies.append(
        pltpu.make_async_copy(diag_hbm.at[pl.ds(1, 1)], diag_ref.at[pl.ds(1, 1)], sems.at[1 + CHUNKS])
    )
    for copy in copies:
        copy.start()
    for copy in lists:
        copy.wait()
    ids_ref[1] = slots_of(dst_ref[...], owner_ref[0], dom_size, diag_ref.shape[1])
    for copy in copies:
        copy.wait()


def fetch(after, src, dst, diag, mats):
    vmem = pl.BlockSpec(memory_space=pltpu.VMEM)
    hbm = pl.BlockSpec(memory_space=pltpu.HBM)
    owner = lax.axis_index("dom").astype(jnp.int32)
    return pl.pallas_call(
        functools.partial(fetch_body, lax.axis_size("dom")),
        out_shape=[
            jax.ShapeDtypeStruct((2, *src.shape), jnp.int32),
            pltpu.VMEM((2, *diag.shape[1:]), diag.dtype),
            pltpu.VMEM((1, *mats.shape[1:]), mats.dtype),
        ],
        in_specs=[pl.BlockSpec(memory_space=pltpu.SMEM), vmem, hbm, hbm, hbm, hbm],
        out_specs=[vmem, vmem, vmem],
        scratch_shapes=[pltpu.VMEM(dst.shape, dst.dtype), pltpu.SemaphoreType.DMA((4 + CHUNKS,))],
        compiler_params=pltpu.CompilerParams(vmem_limit_bytes=1 << 20),
    )(owner[None], after, src, dst, diag, mats)


def per_device(right_sides, diag_inverse, panel_mats, panel_src, panel_dst):
    levels, tiles, group, span = right_sides.shape
    rep_size = lax.axis_size("rep")
    rep = lax.axis_index("rep").astype(jnp.int32)
    cols = group * rep_size
    top = lax.broadcasted_iota(jnp.int32, (2, tiles, cols, span), 0) == 0
    partial = right_sides[0].astype(jnp.bfloat16)
    place = lax.broadcasted_iota(jnp.int32, (levels, tiles, cols, span), 2) // group == rep
    own_rhs = jnp.where(place, jnp.concatenate([right_sides] * rep_size, 2), 0.0)
    ids, early_diag, early_mats = fetch(
        partial,
        *(
            pltpu.with_memory_space_constraint(x, pltpu.HBM)
            for x in (panel_src, panel_dst, diag_inverse, panel_mats)
        ),
    )
    late_diag, late_mats = (
        pltpu.with_memory_space_constraint(x, pltpu.VMEM) for x in (diag_inverse, panel_mats)
    )
    store = []
    results = []
    for level in range(levels):
        last = level + 1 == levels
        parts = [partial] + [along_rep(partial, apart) for apart in APART]
        weights = [early_diag if level < 2 else late_diag, early_mats if level < 1 else late_mats]
        if last:
            return run_solve(
                level, last, rep[None], None, parts, weights[:1], results, right_sides.shape
            )
        solved, stored, handed = run_solve(
            level, last, rep[None], ids, parts, weights, store, right_sides.shape
        )
        results.append(solved)
        store.append(stored)
        own, sibling, far, chip = run_panels(level, ids, weights[1], store)
        handed = jnp.where(top, to_sibling(handed), jnp.zeros_like(handed))
        from_chip = to_next_chip(
            (chip.astype(jnp.float32) + handed.astype(jnp.float32)).astype(jnp.bfloat16)
        )
        from_far = to_far(far)
        across = to_sibling(
            (from_chip[0].astype(jnp.float32) + sibling.astype(jnp.float32)).astype(jnp.bfloat16)
        )
        incoming = sum(piece.astype(jnp.float32) for piece in (own, from_chip[1], from_far, across))
        partial = (own_rhs[level + 1] - incoming).astype(jnp.bfloat16)


def solution(mesh):
    return jax.shard_map(
        per_device,
        mesh=mesh,
        in_specs=(
            P(None, "dom", "rep", None),
            P(None, "dom", None, None),
            P(None, ("dom", "rep"), None, None),
            P(None, ("dom", "rep")),
            P(None, ("dom", "rep")),
        ),
        out_specs=P(None, "dom", "rep", None),
        check_vma=False,
    )
```

```python
import functools

import jax
import jax.numpy as jnp
from jax import lax
from jax.experimental import pallas as pl
from jax.experimental.pallas import tpu as pltpu
from jax.sharding import PartitionSpec as P

HALF = 2
OWN, FAR, SIBLING, HANDED, PASSED, DIRECT = range(6)
GROUPS = 6
APART = (2, 3, 1)
CHUNKS = 4
SLOTS = 3


def dom_permute(value, target):
    size = lax.axis_size("dom")
    return lax.ppermute(value, "dom", [(i, target(i) % size) for i in range(size)])


def to_sibling(value):
    return dom_permute(value, lambda i: i ^ 1)


def to_far(value):
    half = lax.axis_size("dom") // 2
    return dom_permute(value, lambda i: i + half)


def to_next_chip(value):
    return dom_permute(value, lambda i: i + 2 if i % 2 else i - 2)


def along_rep(value, apart):
    return lax.ppermute(value, "rep", [(i, i ^ apart) for i in range(lax.axis_size("rep"))])


def place_columns(parts, rep):
    size = len(parts)
    blocks = [part[...].astype(jnp.float32) for part in parts]
    placed = []
    for index in range(size):
        chosen = blocks[0]
        for block, apart in zip(blocks[1:], APART):
            chosen = jnp.where(rep == index ^ apart, block, chosen)
        placed.append(chosen)
    return placed


def solve_body(level, last, *refs):
    refs = list(refs)
    take = lambda count: [refs.pop(0) for _ in range(count)]
    (rep_ref,) = take(1)
    (ids_ref,) = take(1) if not last else (None,)
    parts = take(4)
    (diag_ref,) = take(1)
    (mats_ref,) = take(1) if not last else (None,)
    prev = take(level)
    (out_ref,) = take(1)
    if not last:
        stored_ref, handed_ref = take(2)
    (solved_scr,) = take(1)
    if not last:
        store_scr, acc_scr, chosen_ref = take(3)
    tiles, cols, _ = solved_scr.shape
    group = cols // 4
    if level == 0:
        for index, block in enumerate(place_columns(parts, rep_ref[0])):
            solved_scr[:, index * group : (index + 1) * group, :] = block
        residuals = [solved_scr[t].astype(jnp.bfloat16) for t in range(tiles)]
    else:
        residuals = [
            sum(part[t].astype(jnp.float32) for part in parts).astype(jnp.bfloat16) for t in range(tiles)
        ]
    for t in range(tiles):
        solved = jnp.dot(residuals[t], diag_ref[0, t], preferred_element_type=jnp.float32)
        solved_scr[t] = solved
        if not last:
            stored_ref[t] = solved.astype(jnp.bfloat16)
            store_scr[level * tiles + t] = solved.astype(jnp.bfloat16)
    own = solved_scr[:, :group, :]
    for other in range(1, cols // group):
        own = jnp.where(rep_ref[0] == other, solved_scr[:, other * group : (other + 1) * group, :], own)
    if last:
        for earlier in range(level):
            out_ref[earlier] = prev[earlier][...]
        out_ref[level] = own
        return
    out_ref[...] = own
    for earlier in range(level):
        for t in range(tiles):
            store_scr[earlier * tiles + t] = prev[earlier][t]
    for r in range(SLOTS):
        chosen_ref[r] = 0
    count = jnp.int32(0)
    for p in range(mats_ref.shape[1]):
        row = ids_ref[1, level, p] - HANDED * tiles
        live = jnp.logical_and(row >= 0, row < tiles)
        chosen_ref[jnp.minimum(count, SLOTS)] = jnp.int32(p)
        count = count + live.astype(jnp.int32)
    acc_scr[...] = jnp.zeros_like(acc_scr)
    for r in range(SLOTS):
        p = chosen_ref[r]
        update = jnp.dot(
            store_scr[ids_ref[0, level, p]], mats_ref[level, p], preferred_element_type=jnp.float32
        )
        row = jnp.where(r < count, ids_ref[1, level, p] - HANDED * tiles, tiles)
        acc_scr[row] = acc_scr[row] + update
    handed_ref[...] = acc_scr[:tiles].astype(jnp.bfloat16)


def panels_body(level, *refs):
    refs = list(refs)
    take = lambda count: [refs.pop(0) for _ in range(count)]
    ids_ref, mats_ref = take(2)
    stores = take(level + 1)
    own_ref, sibling_ref, far_ref, chip_ref, store_scr, acc_scr = refs
    tiles = own_ref.shape[0]
    for earlier in range(level + 1):
        for t in range(tiles):
            store_scr[earlier * tiles + t] = stores[earlier][t]
    acc_scr[...] = jnp.zeros_like(acc_scr)
    for p in range(mats_ref.shape[1]):
        update = jnp.dot(
            store_scr[ids_ref[0, level, p]], mats_ref[level, p], preferred_element_type=jnp.float32
        )
        slot = ids_ref[1, level, p]
        acc_scr[slot] = acc_scr[slot] + update

    def sums(index):
        return acc_scr[index * tiles : (index + 1) * tiles].astype(jnp.bfloat16)

    own_ref[...] = sums(OWN)
    sibling_ref[...] = sums(SIBLING)
    far_ref[...] = sums(FAR)
    chip_ref[0] = sums(PASSED)
    chip_ref[1] = sums(DIRECT)


def run_solve(level, last, rep, ids, parts, weights, prev, shape):
    levels, tiles, group, span = shape
    cols = 4 * group
    smem = pl.BlockSpec(memory_space=pltpu.SMEM)
    vmem = pl.BlockSpec(memory_space=pltpu.VMEM)
    scalars = [rep] if last else [rep, ids]
    inner = [*parts, *weights, *prev]
    scratch = [pltpu.VMEM((tiles, cols, span), jnp.float32)]
    if last:
        outs = jax.ShapeDtypeStruct(shape, jnp.float32)
        out_specs = vmem
    else:
        block = jax.ShapeDtypeStruct((tiles, cols, span), jnp.bfloat16)
        outs = [jax.ShapeDtypeStruct((tiles, group, span), jnp.float32), block, block]
        out_specs = [vmem] * len(outs)
        scratch.append(pltpu.VMEM(((level + 1) * tiles, cols, span), jnp.bfloat16))
        scratch.append(pltpu.VMEM((tiles + 1, cols, span), jnp.float32))
        scratch.append(pltpu.SMEM((SLOTS + 1,), jnp.int32))
    return pl.pallas_call(
        functools.partial(solve_body, level, last),
        out_shape=outs,
        in_specs=[smem] * len(scalars) + [vmem] * len(inner),
        out_specs=out_specs,
        scratch_shapes=scratch,
        compiler_params=pltpu.CompilerParams(vmem_limit_bytes=6 << 20),
    )(*scalars, *inner)


def run_panels(level, ids, mats, stores):
    smem = pl.BlockSpec(memory_space=pltpu.SMEM)
    vmem = pl.BlockSpec(memory_space=pltpu.VMEM)
    tiles, cols, span = stores[0].shape
    return pl.pallas_call(
        functools.partial(panels_body, level),
        out_shape=[
            jax.ShapeDtypeStruct((*lead, tiles, cols, span), jnp.bfloat16) for lead in ((), (), (), (2,))
        ],
        in_specs=[smem] + [vmem] * (1 + len(stores)),
        out_specs=[vmem] * 4,
        scratch_shapes=[
            pltpu.VMEM(((level + 1) * tiles, cols, span), jnp.bfloat16),
            pltpu.VMEM((GROUPS * tiles + 1, cols, span), jnp.float32),
        ],
        compiler_params=pltpu.CompilerParams(vmem_limit_bytes=6 << 20),
    )(ids, mats, *stores)


def slots_of(panel_dst, owner, dom_size, tiles):
    target = jnp.zeros_like(panel_dst)
    for other in range(1, dom_size):
        target = target + (panel_dst >= other * tiles).astype(jnp.int32)
    distance = target - owner
    distance = jnp.where(distance < 0, distance + dom_size, distance)
    near = jnp.where(distance > dom_size // 2, distance - dom_size, distance)
    onward = jnp.where(owner % 2 == 1, near, -near)
    group = jnp.where(
        distance == dom_size // 2,
        FAR,
        jnp.where(
            onward == 0,
            OWN,
            jnp.where(
                onward == 1, PASSED, jnp.where(onward == 2, DIRECT, jnp.where(onward == -1, SIBLING, HANDED))
            ),
        ),
    )
    return jnp.where(panel_dst >= 0, group * tiles + panel_dst - target * tiles, GROUPS * tiles)


def fetch_body(dom_size, *refs):
    owner_ref, _, src_hbm, dst_hbm, diag_hbm, mats_hbm, ids_ref, diag_ref, mats_ref, dst_ref, sems = refs
    lists = [
        pltpu.make_async_copy(src_hbm, ids_ref.at[0], sems.at[1 + CHUNKS]),
        pltpu.make_async_copy(dst_hbm, dst_ref, sems.at[2 + CHUNKS]),
    ]
    for copy in lists:
        copy.start()
    copies = [pltpu.make_async_copy(diag_hbm.at[pl.ds(0, 1)], diag_ref, sems.at[0])]
    step = mats_ref.shape[1] // CHUNKS
    for chunk in range(CHUNKS):
        some = pl.ds(chunk * step, step)
        copies.append(
            pltpu.make_async_copy(mats_hbm.at[pl.ds(0, 1), some], mats_ref.at[:, some], sems.at[1 + chunk])
        )
    for copy in copies:
        copy.start()
    for copy in lists:
        copy.wait()
    ids_ref[1] = slots_of(dst_ref[...], owner_ref[0], dom_size, diag_ref.shape[1])
    for copy in copies:
        copy.wait()


def fetch(after, src, dst, diag, mats):
    vmem = pl.BlockSpec(memory_space=pltpu.VMEM)
    hbm = pl.BlockSpec(memory_space=pltpu.HBM)
    owner = lax.axis_index("dom").astype(jnp.int32)
    return pl.pallas_call(
        functools.partial(fetch_body, lax.axis_size("dom")),
        out_shape=[
            jax.ShapeDtypeStruct((2, *src.shape), jnp.int32),
            pltpu.VMEM((1, *diag.shape[1:]), diag.dtype),
            pltpu.VMEM((1, *mats.shape[1:]), mats.dtype),
        ],
        in_specs=[pl.BlockSpec(memory_space=pltpu.SMEM), vmem, hbm, hbm, hbm, hbm],
        out_specs=[vmem, vmem, vmem],
        scratch_shapes=[pltpu.VMEM(dst.shape, dst.dtype), pltpu.SemaphoreType.DMA((3 + CHUNKS,))],
        compiler_params=pltpu.CompilerParams(vmem_limit_bytes=1 << 20),
    )(owner[None], after, src, dst, diag, mats)


def next_diag_body(level, *refs):
    _, sibling_ref, diag_hbm, passed_ref, diag_ref, sems = refs
    tiles = diag_ref.shape[1]
    copies = [
        pltpu.make_async_copy(diag_hbm.at[pl.ds(level, 1), some], diag_ref.at[:, some], sems.at[half])
        for half, some in enumerate((pl.ds(0, tiles // 2), pl.ds(tiles // 2, tiles // 2)))
    ]
    for copy in copies:
        copy.start()
    passed_ref[...] = sibling_ref[...]
    for copy in copies:
        copy.wait()


def next_diag(level, after, sibling, diag):
    vmem = pl.BlockSpec(memory_space=pltpu.VMEM)
    return pl.pallas_call(
        functools.partial(next_diag_body, level),
        out_shape=[
            jax.ShapeDtypeStruct(sibling.shape, sibling.dtype),
            pltpu.VMEM((1, *diag.shape[1:]), diag.dtype),
        ],
        in_specs=[vmem, vmem, pl.BlockSpec(memory_space=pltpu.HBM)],
        out_specs=[vmem, vmem],
        scratch_shapes=[pltpu.SemaphoreType.DMA((2,))],
        compiler_params=pltpu.CompilerParams(vmem_limit_bytes=1 << 20),
    )(after, sibling, diag)


def per_device(right_sides, diag_inverse, panel_mats, panel_src, panel_dst):
    levels, tiles, group, span = right_sides.shape
    rep_size = lax.axis_size("rep")
    rep = lax.axis_index("rep").astype(jnp.int32)
    cols = group * rep_size
    top = lax.broadcasted_iota(jnp.int32, (2, tiles, cols, span), 0) == 0
    partial = right_sides[0].astype(jnp.bfloat16)
    place = lax.broadcasted_iota(jnp.int32, (levels, tiles, cols, span), 2) // group == rep
    own_rhs = jnp.where(place, jnp.concatenate([right_sides] * rep_size, 2), 0.0)
    src, dst, diag_hbm, mats_hbm = (
        pltpu.with_memory_space_constraint(x, pltpu.HBM)
        for x in (panel_src, panel_dst, diag_inverse, panel_mats)
    )
    ids, diag, early_mats = fetch(partial, src, dst, diag_hbm, mats_hbm)
    late_mats = pltpu.with_memory_space_constraint(panel_mats, pltpu.VMEM)
    store = []
    results = []
    for level in range(levels):
        last = level + 1 == levels
        parts = [partial] + [along_rep(partial, apart) for apart in APART]
        weights = [diag, late_mats if level else early_mats]
        if last:
            return run_solve(
                level, last, rep[None], None, parts, weights[:1], results, right_sides.shape
            )
        solved, stored, handed = run_solve(
            level, last, rep[None], ids, parts, weights, store, right_sides.shape
        )
        results.append(solved)
        store.append(stored)
        own, sibling, far, chip = run_panels(level, ids, weights[1], store)
        handed = jnp.where(top, to_sibling(handed), jnp.zeros_like(handed))
        chip = (chip.astype(jnp.float32) + handed.astype(jnp.float32)).astype(jnp.bfloat16)
        from_chip = to_next_chip(chip)
        sibling, diag = next_diag(level + 1, chip, sibling, diag_hbm)
        from_far = to_far(far)
        across = to_sibling(
            (from_chip[0].astype(jnp.float32) + sibling.astype(jnp.float32)).astype(jnp.bfloat16)
        )
        incoming = sum(piece.astype(jnp.float32) for piece in (own, from_chip[1], from_far, across))
        partial = (own_rhs[level + 1] - incoming).astype(jnp.bfloat16)


def solution(mesh):
    return jax.shard_map(
        per_device,
        mesh=mesh,
        in_specs=(
            P(None, "dom", "rep", None),
            P(None, "dom", None, None),
            P(None, ("dom", "rep"), None, None),
            P(None, ("dom", "rep")),
            P(None, ("dom", "rep")),
        ),
        out_specs=P(None, "dom", "rep", None),
        check_vma=False,
    )
```

```python
import functools

import jax
import jax.numpy as jnp
from jax import lax
from jax.experimental import pallas as pl
from jax.experimental.pallas import tpu as pltpu
from jax.sharding import PartitionSpec as P

HALF = 2
OWN, FAR, SIBLING, HANDED, PASSED, DIRECT = range(6)
GROUPS = 6
APART = (2, 3, 1)
APART_FIRST = (3, 2, 1)
CHUNKS = 4
SLOTS = 3
WIDE = 256


def dom_permute(value, target):
    size = lax.axis_size("dom")
    return lax.ppermute(value, "dom", [(i, target(i) % size) for i in range(size)])


def to_sibling(value):
    return dom_permute(value, lambda i: i ^ 1)


def to_far(value):
    half = lax.axis_size("dom") // 2
    return dom_permute(value, lambda i: i + half)


def to_next_chip(value):
    return dom_permute(value, lambda i: i + 1 if i % 2 else i - 1)


def along_rep(value, apart):
    return lax.ppermute(value, "rep", [(i, i ^ apart) for i in range(lax.axis_size("rep"))])


def place_columns(parts, rep):
    size = len(parts)
    blocks = [part[...].astype(jnp.float32) for part in parts]
    placed = []
    for index in range(size):
        chosen = blocks[0]
        for block, apart in zip(blocks[1:], APART_FIRST):
            chosen = jnp.where(rep == index ^ apart, block, chosen)
        placed.append(chosen)
    return placed


def two_products(left, right, left_matrix, right_matrix):
    rows, span = left.shape
    main = span // WIDE * WIDE
    rest = span - main
    dot = functools.partial(jnp.dot, preferred_element_type=jnp.float32)
    tail = dot(
        jnp.concatenate([left, right], 0),
        jnp.concatenate([left_matrix[:, main:], right_matrix[:, main:]], 1),
    )
    return (
        jnp.concatenate([dot(left, left_matrix[:, :main]), tail[:rows, :rest]], 1),
        jnp.concatenate([dot(right, right_matrix[:, :main]), tail[rows:, rest:]], 1),
    )


def solve_body(level, last, *refs):
    refs = list(refs)
    take = lambda count: [refs.pop(0) for _ in range(count)]
    (rep_ref,) = take(1)
    (ids_ref,) = take(1) if not last else (None,)
    parts = take(4)
    (diag_ref,) = take(1)
    (mats_ref,) = take(1) if not last else (None,)
    prev = take(level)
    (out_ref,) = take(1)
    if not last:
        stored_ref, handed_ref = take(2)
    (solved_scr,) = take(1)
    if not last:
        store_scr, acc_scr, chosen_ref = take(3)
    tiles, cols, _ = solved_scr.shape
    group = cols // 4
    if level == 0:
        for index, block in enumerate(place_columns(parts, rep_ref[0])):
            solved_scr[:, index * group : (index + 1) * group, :] = block
        residuals = [solved_scr[t].astype(jnp.bfloat16) for t in range(tiles)]
    else:
        residuals = [
            sum(part[t].astype(jnp.float32) for part in parts).astype(jnp.bfloat16) for t in range(tiles)
        ]
    products = []
    for t in range(0, tiles, 2):
        products += two_products(residuals[t], residuals[t + 1], diag_ref[0, t], diag_ref[0, t + 1])
    for t, solved in enumerate(products):
        solved_scr[t] = solved
        if not last:
            stored_ref[t] = solved.astype(jnp.bfloat16)
            store_scr[level * tiles + t] = solved.astype(jnp.bfloat16)
    own = solved_scr[:, :group, :]
    for other in range(1, cols // group):
        own = jnp.where(rep_ref[0] == other, solved_scr[:, other * group : (other + 1) * group, :], own)
    if last:
        for earlier in range(level):
            out_ref[earlier] = prev[earlier][...]
        out_ref[level] = own
        return
    out_ref[...] = own
    for earlier in range(level):
        for t in range(tiles):
            store_scr[earlier * tiles + t] = prev[earlier][t]
    for r in range(SLOTS):
        chosen_ref[r] = 0
    count = jnp.int32(0)
    for p in range(mats_ref.shape[1]):
        row = ids_ref[1, level, p] - HANDED * tiles
        live = jnp.logical_and(row >= 0, row < tiles)
        chosen_ref[jnp.minimum(count, SLOTS)] = jnp.int32(p)
        count = count + live.astype(jnp.int32)
    acc_scr[...] = jnp.zeros_like(acc_scr)
    for r in range(SLOTS):
        p = chosen_ref[r]
        update = jnp.dot(
            store_scr[ids_ref[0, level, p]], mats_ref[level, p], preferred_element_type=jnp.float32
        )
        row = jnp.where(r < count, ids_ref[1, level, p] - HANDED * tiles, tiles)
        acc_scr[row] = acc_scr[row] + update
    handed_ref[...] = acc_scr[:tiles].astype(jnp.bfloat16)


def panels_body(level, *refs):
    refs = list(refs)
    take = lambda count: [refs.pop(0) for _ in range(count)]
    ids_ref, mats_ref = take(2)
    stores = take(level + 1)
    own_ref, sibling_ref, far_ref, chip_ref, store_scr, updates_scr, acc_scr = refs
    tiles = own_ref.shape[0]
    for earlier in range(level + 1):
        for t in range(tiles):
            store_scr[earlier * tiles + t] = stores[earlier][t]
    for p in range(0, mats_ref.shape[1], 2):
        updates_scr[p], updates_scr[p + 1] = two_products(
            store_scr[ids_ref[0, level, p]],
            store_scr[ids_ref[0, level, p + 1]],
            mats_ref[level, p],
            mats_ref[level, p + 1],
        )
    acc_scr[...] = jnp.zeros_like(acc_scr)
    for p in range(mats_ref.shape[1]):
        slot = ids_ref[1, level, p]
        acc_scr[slot] = acc_scr[slot] + updates_scr[p]

    def sums(index):
        return acc_scr[index * tiles : (index + 1) * tiles].astype(jnp.bfloat16)

    own_ref[...] = sums(OWN)
    sibling_ref[...] = sums(SIBLING)
    far_ref[...] = sums(FAR)
    chip_ref[0] = sums(PASSED)
    chip_ref[1] = sums(DIRECT)


def run_solve(level, last, rep, ids, parts, weights, prev, shape):
    levels, tiles, group, span = shape
    cols = 4 * group
    smem = pl.BlockSpec(memory_space=pltpu.SMEM)
    vmem = pl.BlockSpec(memory_space=pltpu.VMEM)
    scalars = [rep] if last else [rep, ids]
    inner = [*parts, *weights, *prev]
    scratch = [pltpu.VMEM((tiles, cols, span), jnp.float32)]
    if last:
        outs = jax.ShapeDtypeStruct(shape, jnp.float32)
        out_specs = vmem
    else:
        block = jax.ShapeDtypeStruct((tiles, cols, span), jnp.bfloat16)
        outs = [jax.ShapeDtypeStruct((tiles, group, span), jnp.float32), block, block]
        out_specs = [vmem] * len(outs)
        scratch.append(pltpu.VMEM(((level + 1) * tiles, cols, span), jnp.bfloat16))
        scratch.append(pltpu.VMEM((tiles + 1, cols, span), jnp.float32))
        scratch.append(pltpu.SMEM((SLOTS + 1,), jnp.int32))
    return pl.pallas_call(
        functools.partial(solve_body, level, last),
        out_shape=outs,
        in_specs=[smem] * len(scalars) + [vmem] * len(inner),
        out_specs=out_specs,
        scratch_shapes=scratch,
        compiler_params=pltpu.CompilerParams(vmem_limit_bytes=6 << 20),
    )(*scalars, *inner)


def run_panels(level, ids, mats, stores):
    smem = pl.BlockSpec(memory_space=pltpu.SMEM)
    vmem = pl.BlockSpec(memory_space=pltpu.VMEM)
    tiles, cols, span = stores[0].shape
    return pl.pallas_call(
        functools.partial(panels_body, level),
        out_shape=[
            jax.ShapeDtypeStruct((*lead, tiles, cols, span), jnp.bfloat16) for lead in ((), (), (), (2,))
        ],
        in_specs=[smem] + [vmem] * (1 + len(stores)),
        out_specs=[vmem] * 4,
        scratch_shapes=[
            pltpu.VMEM(((level + 1) * tiles, cols, span), jnp.bfloat16),
            pltpu.VMEM((mats.shape[1], cols, span), jnp.float32),
            pltpu.VMEM((GROUPS * tiles + 1, cols, span), jnp.float32),
        ],
        compiler_params=pltpu.CompilerParams(vmem_limit_bytes=6 << 20),
    )(ids, mats, *stores)


def slots_of(panel_dst, owner, dom_size, tiles):
    target = jnp.zeros_like(panel_dst)
    for other in range(1, dom_size):
        target = target + (panel_dst >= other * tiles).astype(jnp.int32)
    distance = target - owner
    distance = jnp.where(distance < 0, distance + dom_size, distance)
    near = jnp.where(distance > dom_size // 2, distance - dom_size, distance)
    onward = jnp.where(owner % 2 == 1, near, -near)
    group = jnp.where(
        distance == dom_size // 2,
        FAR,
        jnp.where(
            onward == 0,
            OWN,
            jnp.where(
                onward == 1, PASSED, jnp.where(onward == 2, DIRECT, jnp.where(onward == -1, SIBLING, HANDED))
            ),
        ),
    )
    return jnp.where(panel_dst >= 0, group * tiles + panel_dst - target * tiles, GROUPS * tiles)


def fetch_body(dom_size, *refs):
    owner_ref, _, src_hbm, dst_hbm, diag_hbm, mats_hbm, ids_ref, diag_ref, mats_ref, dst_ref, sems = refs
    lists = [
        pltpu.make_async_copy(src_hbm, ids_ref.at[0], sems.at[1 + CHUNKS]),
        pltpu.make_async_copy(dst_hbm, dst_ref, sems.at[2 + CHUNKS]),
    ]
    for copy in lists:
        copy.start()
    copies = [pltpu.make_async_copy(diag_hbm.at[pl.ds(0, 1)], diag_ref, sems.at[0])]
    step = mats_ref.shape[1] // CHUNKS
    for chunk in range(CHUNKS):
        some = pl.ds(chunk * step, step)
        copies.append(
            pltpu.make_async_copy(mats_hbm.at[pl.ds(0, 1), some], mats_ref.at[:, some], sems.at[1 + chunk])
        )
    for copy in copies:
        copy.start()
    for copy in lists:
        copy.wait()
    ids_ref[1] = slots_of(dst_ref[...], owner_ref[0], dom_size, diag_ref.shape[1])
    for copy in copies:
        copy.wait()


def fetch(after, src, dst, diag, mats):
    vmem = pl.BlockSpec(memory_space=pltpu.VMEM)
    hbm = pl.BlockSpec(memory_space=pltpu.HBM)
    owner = lax.axis_index("dom").astype(jnp.int32)
    return pl.pallas_call(
        functools.partial(fetch_body, lax.axis_size("dom")),
        out_shape=[
            jax.ShapeDtypeStruct((2, *src.shape), jnp.int32),
            pltpu.VMEM((1, *diag.shape[1:]), diag.dtype),
            pltpu.VMEM((1, *mats.shape[1:]), mats.dtype),
        ],
        in_specs=[pl.BlockSpec(memory_space=pltpu.SMEM), vmem, hbm, hbm, hbm, hbm],
        out_specs=[vmem, vmem, vmem],
        scratch_shapes=[pltpu.VMEM(dst.shape, dst.dtype), pltpu.SemaphoreType.DMA((3 + CHUNKS,))],
        compiler_params=pltpu.CompilerParams(vmem_limit_bytes=1 << 20),
    )(owner[None], after, src, dst, diag, mats)


def next_diag_body(level, *refs):
    _, sibling_ref, diag_hbm, passed_ref, diag_ref, sems = refs
    tiles = diag_ref.shape[1]
    copies = [
        pltpu.make_async_copy(diag_hbm.at[pl.ds(level, 1), some], diag_ref.at[:, some], sems.at[half])
        for half, some in enumerate((pl.ds(0, tiles // 2), pl.ds(tiles // 2, tiles // 2)))
    ]
    for copy in copies:
        copy.start()
    passed_ref[...] = sibling_ref[...]
    for copy in copies:
        copy.wait()


def next_diag(level, after, sibling, diag):
    vmem = pl.BlockSpec(memory_space=pltpu.VMEM)
    return pl.pallas_call(
        functools.partial(next_diag_body, level),
        out_shape=[
            jax.ShapeDtypeStruct(sibling.shape, sibling.dtype),
            pltpu.VMEM((1, *diag.shape[1:]), diag.dtype),
        ],
        in_specs=[vmem, vmem, pl.BlockSpec(memory_space=pltpu.HBM)],
        out_specs=[vmem, vmem],
        scratch_shapes=[pltpu.SemaphoreType.DMA((2,))],
        compiler_params=pltpu.CompilerParams(vmem_limit_bytes=1 << 20),
    )(after, sibling, diag)


def per_device(right_sides, diag_inverse, panel_mats, panel_src, panel_dst):
    levels, tiles, group, span = right_sides.shape
    rep_size = lax.axis_size("rep")
    rep = lax.axis_index("rep").astype(jnp.int32)
    cols = group * rep_size
    top = lax.broadcasted_iota(jnp.int32, (2, tiles, cols, span), 0) == 0
    partial = right_sides[0].astype(jnp.bfloat16)
    place = lax.broadcasted_iota(jnp.int32, (levels, tiles, cols, span), 2) // group == rep
    own_rhs = jnp.where(place, jnp.concatenate([right_sides] * rep_size, 2), 0.0)
    src, dst, diag_hbm, mats_hbm = (
        pltpu.with_memory_space_constraint(x, pltpu.HBM)
        for x in (panel_src, panel_dst, diag_inverse, panel_mats)
    )
    ids, diag, early_mats = fetch(partial, src, dst, diag_hbm, mats_hbm)
    late_mats = pltpu.with_memory_space_constraint(panel_mats, pltpu.VMEM)
    store = []
    results = []
    for level in range(levels):
        last = level + 1 == levels
        parts = [partial] + [
            along_rep(partial, apart) for apart in (APART if level else APART_FIRST)
        ]
        weights = [diag, late_mats if level else early_mats]
        if last:
            return run_solve(
                level, last, rep[None], None, parts, weights[:1], results, right_sides.shape
            )
        solved, stored, handed = run_solve(
            level, last, rep[None], ids, parts, weights, store, right_sides.shape
        )
        results.append(solved)
        store.append(stored)
        own, sibling, far, chip = run_panels(level, ids, weights[1], store)
        handed = jnp.where(top, to_sibling(handed), jnp.zeros_like(handed))
        chip = (chip.astype(jnp.float32) + handed.astype(jnp.float32)).astype(jnp.bfloat16)
        from_chip = to_next_chip(chip)
        sibling, diag = next_diag(level + 1, chip, sibling, diag_hbm)
        from_far = to_far(far)
        across = to_sibling(
            (from_chip[1].astype(jnp.float32) + sibling.astype(jnp.float32)).astype(jnp.bfloat16)
        )
        incoming = sum(piece.astype(jnp.float32) for piece in (own, from_chip[0], from_far, across))
        partial = (own_rhs[level + 1] - incoming).astype(jnp.bfloat16)


def solution(mesh):
    return jax.shard_map(
        per_device,
        mesh=mesh,
        in_specs=(
            P(None, "dom", "rep", None),
            P(None, "dom", None, None),
            P(None, ("dom", "rep"), None, None),
            P(None, ("dom", "rep")),
            P(None, ("dom", "rep")),
        ),
        out_specs=P(None, "dom", "rep", None),
        check_vma=False,
    )
```

```python
import functools

import jax
import jax.numpy as jnp
from jax import lax
from jax.experimental import pallas as pl
from jax.experimental.pallas import tpu as pltpu
from jax.sharding import PartitionSpec as P

HALF = 2
OWN, FAR, SIBLING, HANDED, PASSED, DIRECT = range(6)
GROUPS = 6
APART = (2, 3, 1)
APART_FIRST = (3, 2, 1)
CHUNKS = 4
SLOTS = 3
WIDE = 256


def dom_permute(value, target):
    size = lax.axis_size("dom")
    return lax.ppermute(value, "dom", [(i, target(i) % size) for i in range(size)])


def to_sibling(value):
    return dom_permute(value, lambda i: i ^ 1)


def to_far(value):
    half = lax.axis_size("dom") // 2
    return dom_permute(value, lambda i: i + half)


def to_next_chip(value):
    return dom_permute(value, lambda i: i + 1 if i % 2 else i - 1)


def along_rep(value, apart):
    return lax.ppermute(value, "rep", [(i, i ^ apart) for i in range(lax.axis_size("rep"))])


def place_columns(parts, rep):
    size = len(parts)
    blocks = [part[...].astype(jnp.float32) for part in parts]
    placed = []
    for index in range(size):
        chosen = blocks[0]
        for block, apart in zip(blocks[1:], APART_FIRST):
            chosen = jnp.where(rep == index ^ apart, block, chosen)
        placed.append(chosen)
    return placed


def two_products(left, right, left_matrix, right_matrix):
    rows, span = left.shape
    main = span // WIDE * WIDE
    rest = span - main
    dot = functools.partial(jnp.dot, preferred_element_type=jnp.float32)
    tail = dot(
        jnp.concatenate([left, right], 0),
        jnp.concatenate([left_matrix[:, main:], right_matrix[:, main:]], 1),
    )
    return (
        jnp.concatenate([dot(left, left_matrix[:, :main]), tail[:rows, :rest]], 1),
        jnp.concatenate([dot(right, right_matrix[:, :main]), tail[rows:, rest:]], 1),
    )


def solve_body(level, last, *refs):
    refs = list(refs)
    take = lambda count: [refs.pop(0) for _ in range(count)]
    (rep_ref,) = take(1)
    (ids_ref,) = take(1) if not last else (None,)
    parts = take(4)
    (diag_ref,) = take(1)
    (mats_ref,) = take(1) if not last else (None,)
    prev = take(level)
    (out_ref,) = take(1)
    if not last:
        stored_ref, handed_ref = take(2)
    (solved_scr,) = take(1)
    if not last:
        store_scr, acc_scr, chosen_ref = take(3)
    tiles, cols, _ = solved_scr.shape
    group = cols // 4
    if level == 0:
        for index, block in enumerate(place_columns(parts, rep_ref[0])):
            solved_scr[:, index * group : (index + 1) * group, :] = block
        residuals = [solved_scr[t].astype(jnp.bfloat16) for t in range(tiles)]
    else:
        residuals = [
            sum(part[t].astype(jnp.float32) for part in parts).astype(jnp.bfloat16) for t in range(tiles)
        ]
    products = []
    for t in range(0, tiles, 2):
        products += two_products(residuals[t], residuals[t + 1], diag_ref[0, t], diag_ref[0, t + 1])
    for t, solved in enumerate(products):
        solved_scr[t] = solved
        if not last:
            stored_ref[t] = solved.astype(jnp.bfloat16)
            store_scr[level * tiles + t] = solved.astype(jnp.bfloat16)
    own = solved_scr[:, :group, :]
    for other in range(1, cols // group):
        own = jnp.where(rep_ref[0] == other, solved_scr[:, other * group : (other + 1) * group, :], own)
    if last:
        for earlier in range(level):
            out_ref[earlier] = prev[earlier][...]
        out_ref[level] = own
        return
    out_ref[...] = own
    for earlier in range(level):
        for t in range(tiles):
            store_scr[earlier * tiles + t] = prev[earlier][t]
    for r in range(SLOTS):
        chosen_ref[r] = 0
    count = jnp.int32(0)
    for p in range(mats_ref.shape[1]):
        row = ids_ref[1, p] - HANDED * tiles
        live = jnp.logical_and(row >= 0, row < tiles)
        chosen_ref[jnp.minimum(count, SLOTS)] = jnp.int32(p)
        count = count + live.astype(jnp.int32)
    acc_scr[...] = jnp.zeros_like(acc_scr)
    for r in range(SLOTS):
        p = chosen_ref[r]
        update = jnp.dot(
            store_scr[ids_ref[0, p]], mats_ref[level, p], preferred_element_type=jnp.float32
        )
        row = jnp.where(r < count, ids_ref[1, p] - HANDED * tiles, tiles)
        acc_scr[row] = acc_scr[row] + update
    handed_ref[...] = acc_scr[:tiles].astype(jnp.bfloat16)


def panels_body(level, *refs):
    refs = list(refs)
    take = lambda count: [refs.pop(0) for _ in range(count)]
    ids_ref, mats_ref = take(2)
    stores = take(level + 1)
    own_ref, sibling_ref, far_ref, chip_ref, store_scr, updates_scr, acc_scr = refs
    tiles = own_ref.shape[0]
    for earlier in range(level + 1):
        for t in range(tiles):
            store_scr[earlier * tiles + t] = stores[earlier][t]
    for p in range(0, mats_ref.shape[1], 2):
        updates_scr[p], updates_scr[p + 1] = two_products(
            store_scr[ids_ref[0, p]],
            store_scr[ids_ref[0, p + 1]],
            mats_ref[level, p],
            mats_ref[level, p + 1],
        )
    acc_scr[...] = jnp.zeros_like(acc_scr)
    for p in range(mats_ref.shape[1]):
        slot = ids_ref[1, p]
        acc_scr[slot] = acc_scr[slot] + updates_scr[p]

    def sums(index):
        return acc_scr[index * tiles : (index + 1) * tiles].astype(jnp.bfloat16)

    own_ref[...] = sums(OWN)
    sibling_ref[...] = sums(SIBLING)
    far_ref[...] = sums(FAR)
    chip_ref[0] = sums(PASSED)
    chip_ref[1] = sums(DIRECT)


def last_body(*refs):
    *refs, out_ref = refs
    parts, diag_ref, earlier = refs[:4], refs[4], refs[5:]
    for level, ref in enumerate(earlier):
        out_ref[level] = ref[...]
    for t in range(diag_ref.shape[1]):
        residual = sum(part[t].astype(jnp.float32) for part in parts).astype(jnp.bfloat16)
        out_ref[len(earlier), t] = jnp.dot(residual, diag_ref[0, t], preferred_element_type=jnp.float32)


def run_last(parts, diag, results, shape):
    vmem = pl.BlockSpec(memory_space=pltpu.VMEM)
    args = [*parts, diag, *results]
    return pl.pallas_call(
        last_body,
        out_shape=jax.ShapeDtypeStruct(shape, jnp.float32),
        in_specs=[vmem] * len(args),
        out_specs=vmem,
        compiler_params=pltpu.CompilerParams(vmem_limit_bytes=6 << 20),
    )(*args)


def run_solve(level, last, rep, ids, parts, weights, prev, shape):
    levels, tiles, group, span = shape
    cols = 4 * group
    smem = pl.BlockSpec(memory_space=pltpu.SMEM)
    vmem = pl.BlockSpec(memory_space=pltpu.VMEM)
    scalars = [rep] if last else [rep, ids]
    inner = [*parts, *weights, *prev]
    scratch = [pltpu.VMEM((tiles, cols, span), jnp.float32)]
    if last:
        outs = jax.ShapeDtypeStruct(shape, jnp.float32)
        out_specs = vmem
    else:
        block = jax.ShapeDtypeStruct((tiles, cols, span), jnp.bfloat16)
        outs = [jax.ShapeDtypeStruct((tiles, group, span), jnp.float32), block, block]
        out_specs = [vmem] * len(outs)
        scratch.append(pltpu.VMEM(((level + 1) * tiles, cols, span), jnp.bfloat16))
        scratch.append(pltpu.VMEM((tiles + 1, cols, span), jnp.float32))
        scratch.append(pltpu.SMEM((SLOTS + 1,), jnp.int32))
    return pl.pallas_call(
        functools.partial(solve_body, level, last),
        out_shape=outs,
        in_specs=[smem] * len(scalars) + [vmem] * len(inner),
        out_specs=out_specs,
        scratch_shapes=scratch,
        compiler_params=pltpu.CompilerParams(vmem_limit_bytes=6 << 20),
    )(*scalars, *inner)


def run_panels(level, ids, mats, stores):
    smem = pl.BlockSpec(memory_space=pltpu.SMEM)
    vmem = pl.BlockSpec(memory_space=pltpu.VMEM)
    tiles, cols, span = stores[0].shape
    return pl.pallas_call(
        functools.partial(panels_body, level),
        out_shape=[
            jax.ShapeDtypeStruct((*lead, tiles, cols, span), jnp.bfloat16) for lead in ((), (), (), (2,))
        ],
        in_specs=[smem] + [vmem] * (1 + len(stores)),
        out_specs=[vmem] * 4,
        scratch_shapes=[
            pltpu.VMEM(((level + 1) * tiles, cols, span), jnp.bfloat16),
            pltpu.VMEM((mats.shape[1], cols, span), jnp.float32),
            pltpu.VMEM((GROUPS * tiles + 1, cols, span), jnp.float32),
        ],
        compiler_params=pltpu.CompilerParams(vmem_limit_bytes=6 << 20),
    )(ids, mats, *stores)


def slots_of(panel_dst, owner, dom_size, tiles):
    target = jnp.zeros_like(panel_dst)
    for other in range(1, dom_size):
        target = target + (panel_dst >= other * tiles).astype(jnp.int32)
    distance = target - owner
    distance = jnp.where(distance < 0, distance + dom_size, distance)
    near = jnp.where(distance > dom_size // 2, distance - dom_size, distance)
    onward = jnp.where(owner % 2 == 1, near, -near)
    group = jnp.where(
        distance == dom_size // 2,
        FAR,
        jnp.where(
            onward == 0,
            OWN,
            jnp.where(
                onward == 1, PASSED, jnp.where(onward == 2, DIRECT, jnp.where(onward == -1, SIBLING, HANDED))
            ),
        ),
    )
    return jnp.where(panel_dst >= 0, group * tiles + panel_dst - target * tiles, GROUPS * tiles)


def fetch_body(dom_size, *refs):
    owner_ref, _, src_hbm, dst_hbm, diag_hbm, mats_hbm, *ids_refs, diag_ref, mats_ref, src_ref, dst_ref, sems = refs
    lists = [
        pltpu.make_async_copy(src_hbm, src_ref, sems.at[1 + CHUNKS]),
        pltpu.make_async_copy(dst_hbm, dst_ref, sems.at[2 + CHUNKS]),
    ]
    for copy in lists:
        copy.start()
    copies = [pltpu.make_async_copy(diag_hbm.at[pl.ds(0, 1)], diag_ref, sems.at[0])]
    step = mats_ref.shape[1] // CHUNKS
    for chunk in range(CHUNKS):
        some = pl.ds(chunk * step, step)
        copies.append(
            pltpu.make_async_copy(mats_hbm.at[pl.ds(0, 1), some], mats_ref.at[:, some], sems.at[1 + chunk])
        )
    for copy in copies:
        copy.start()
    for copy in lists:
        copy.wait()
    slots = slots_of(dst_ref[...], owner_ref[0], dom_size, diag_ref.shape[1])
    for level, ids_ref in enumerate(ids_refs):
        ids_ref[0:1] = src_ref[level : level + 1]
        ids_ref[1:2] = slots[level : level + 1]
    for copy in copies:
        copy.wait()


def fetch(after, src, dst, diag, mats):
    vmem = pl.BlockSpec(memory_space=pltpu.VMEM)
    hbm = pl.BlockSpec(memory_space=pltpu.HBM)
    owner = lax.axis_index("dom").astype(jnp.int32)
    return pl.pallas_call(
        functools.partial(fetch_body, lax.axis_size("dom")),
        out_shape=[
            *[jax.ShapeDtypeStruct((2, src.shape[1]), jnp.int32) for _ in range(src.shape[0])],
            pltpu.VMEM((1, *diag.shape[1:]), diag.dtype),
            pltpu.VMEM((1, *mats.shape[1:]), mats.dtype),
        ],
        in_specs=[pl.BlockSpec(memory_space=pltpu.SMEM), vmem, hbm, hbm, hbm, hbm],
        out_specs=[vmem] * (2 + src.shape[0]),
        scratch_shapes=[pltpu.VMEM(src.shape, src.dtype), pltpu.VMEM(dst.shape, dst.dtype), pltpu.SemaphoreType.DMA((3 + CHUNKS,))],
        compiler_params=pltpu.CompilerParams(vmem_limit_bytes=1 << 20),
    )(owner[None], after, src, dst, diag, mats)


def next_diag_body(level, *refs):
    _, sibling_ref, diag_hbm, passed_ref, diag_ref, sems = refs
    tiles = diag_ref.shape[1]
    copies = [
        pltpu.make_async_copy(diag_hbm.at[pl.ds(level, 1), some], diag_ref.at[:, some], sems.at[half])
        for half, some in enumerate((pl.ds(0, tiles // 2), pl.ds(tiles // 2, tiles // 2)))
    ]
    for copy in copies:
        copy.start()
    passed_ref[...] = sibling_ref[...]
    for copy in copies:
        copy.wait()


def next_diag(level, after, sibling, diag):
    vmem = pl.BlockSpec(memory_space=pltpu.VMEM)
    return pl.pallas_call(
        functools.partial(next_diag_body, level),
        out_shape=[
            jax.ShapeDtypeStruct(sibling.shape, sibling.dtype),
            pltpu.VMEM((1, *diag.shape[1:]), diag.dtype),
        ],
        in_specs=[vmem, vmem, pl.BlockSpec(memory_space=pltpu.HBM)],
        out_specs=[vmem, vmem],
        scratch_shapes=[pltpu.SemaphoreType.DMA((2,))],
        compiler_params=pltpu.CompilerParams(vmem_limit_bytes=1 << 20),
    )(after, sibling, diag)


def per_device(right_sides, diag_inverse, panel_mats, panel_src, panel_dst):
    levels, tiles, group, span = right_sides.shape
    rep_size = lax.axis_size("rep")
    rep = lax.axis_index("rep").astype(jnp.int32)
    cols = group * rep_size
    top = lax.broadcasted_iota(jnp.int32, (2, tiles, cols, span), 0) == 0
    partial = right_sides[0].astype(jnp.bfloat16)
    place = lax.broadcasted_iota(jnp.int32, (levels, tiles, cols, span), 2) // group == rep
    own_rhs = jnp.where(place, jnp.concatenate([right_sides] * rep_size, 2), 0.0)
    src, dst, diag_hbm, mats_hbm = (
        pltpu.with_memory_space_constraint(x, pltpu.HBM)
        for x in (panel_src, panel_dst, diag_inverse, panel_mats)
    )
    *ids, diag, early_mats = fetch(partial, src, dst, diag_hbm, mats_hbm)
    late_mats = pltpu.with_memory_space_constraint(panel_mats, pltpu.VMEM)
    store = []
    results = []
    for level in range(levels):
        last = level + 1 == levels
        if last:
            pieces = [
                sum(
                    jnp.where(rep ^ apart == index, full[:, index * group : (index + 1) * group], 0.0)
                    for index in range(rep_size)
                ).astype(jnp.bfloat16)
                for apart in (0, *APART)
            ]
            parts = pieces[:1] + [along_rep(piece, apart) for piece, apart in zip(pieces[1:], APART)]
            return run_last(parts, diag, results, right_sides.shape)
        parts = [partial] + [
            along_rep(partial, apart) for apart in (APART if level else APART_FIRST)
        ]
        weights = [diag, late_mats if level else early_mats]
        solved, stored, handed = run_solve(
            level, last, rep[None], ids[level], parts, weights, store, right_sides.shape
        )
        results.append(solved)
        store.append(stored)
        own, sibling, far, chip = run_panels(level, ids[level], weights[1], store)
        handed = jnp.where(top, to_sibling(handed), jnp.zeros_like(handed))
        chip = (chip.astype(jnp.float32) + handed.astype(jnp.float32)).astype(jnp.bfloat16)
        from_chip = to_next_chip(chip)
        sibling, diag = next_diag(level + 1, chip, sibling, diag_hbm)
        from_far = to_far(far)
        across = to_sibling(
            (from_chip[1].astype(jnp.float32) + sibling.astype(jnp.float32)).astype(jnp.bfloat16)
        )
        incoming = sum(piece.astype(jnp.float32) for piece in (own, from_chip[0], from_far, across))
        full = own_rhs[level + 1] - incoming
        partial = full.astype(jnp.bfloat16)


def solution(mesh):
    return jax.shard_map(
        per_device,
        mesh=mesh,
        in_specs=(
            P(None, "dom", "rep", None),
            P(None, "dom", None, None),
            P(None, ("dom", "rep"), None, None),
            P(None, ("dom", "rep")),
            P(None, ("dom", "rep")),
        ),
        out_specs=P(None, "dom", "rep", None),
        check_vma=False,
    )
```

```python
import functools

import jax
import jax.numpy as jnp
from jax import lax
from jax.experimental import pallas as pl
from jax.experimental.pallas import tpu as pltpu
from jax.sharding import PartitionSpec as P

HALF = 2
OWN, FAR, SIBLING, HANDED, PASSED, DIRECT = range(6)
GROUPS = 6
APART = (2, 3, 1)
APART_FIRST = (3, 2, 1)
CHUNKS = 4
SLOTS = 3
WIDE = 256


def dom_permute(value, target):
    size = lax.axis_size("dom")
    return lax.ppermute(value, "dom", [(i, target(i) % size) for i in range(size)])


def to_sibling(value):
    return dom_permute(value, lambda i: i ^ 1)


def to_far(value):
    half = lax.axis_size("dom") // 2
    return dom_permute(value, lambda i: i + half)


def to_next_chip(value):
    return dom_permute(value, lambda i: i + 1 if i % 2 else i - 1)


def along_rep(value, apart):
    return lax.ppermute(value, "rep", [(i, i ^ apart) for i in range(lax.axis_size("rep"))])


def place_columns(parts, rep):
    size = len(parts)
    blocks = [part[...].astype(jnp.float32) for part in parts]
    placed = []
    for index in range(size):
        chosen = blocks[0]
        for block, apart in zip(blocks[1:], APART_FIRST):
            chosen = jnp.where(rep == index ^ apart, block, chosen)
        placed.append(chosen)
    return placed


def two_products(left, right, left_matrix, right_matrix):
    rows, span = left.shape
    main = span // WIDE * WIDE
    rest = span - main
    dot = functools.partial(jnp.dot, preferred_element_type=jnp.float32)
    tail = dot(
        jnp.concatenate([left, right], 0),
        jnp.concatenate([left_matrix[:, main:], right_matrix[:, main:]], 1),
    )
    return (
        jnp.concatenate([dot(left, left_matrix[:, :main]), tail[:rows, :rest]], 1),
        jnp.concatenate([dot(right, right_matrix[:, :main]), tail[rows:, rest:]], 1),
    )


def solve_body(level, last, *refs):
    refs = list(refs)
    take = lambda count: [refs.pop(0) for _ in range(count)]
    (rep_ref,) = take(1)
    (ids_ref,) = take(1) if not last else (None,)
    parts = take(4)
    (diag_ref,) = take(1)
    (mats_ref,) = take(1) if not last else (None,)
    prev = take(level)
    (out_ref,) = take(1)
    if not last:
        stored_ref, handed_ref = take(2)
    (solved_scr,) = take(1)
    if not last:
        store_scr, acc_scr, chosen_ref = take(3)
    tiles, cols, _ = solved_scr.shape
    group = cols // 4
    if level == 0:
        for index, block in enumerate(place_columns(parts, rep_ref[0])):
            solved_scr[:, index * group : (index + 1) * group, :] = block
        residuals = [solved_scr[t].astype(jnp.bfloat16) for t in range(tiles)]
    else:
        residuals = [
            sum(part[t].astype(jnp.float32) for part in parts).astype(jnp.bfloat16) for t in range(tiles)
        ]
    products = []
    for t in range(0, tiles, 2):
        products += two_products(residuals[t], residuals[t + 1], diag_ref[0, t], diag_ref[0, t + 1])
    for t, solved in enumerate(products):
        solved_scr[t] = solved
        if not last:
            stored_ref[t] = solved.astype(jnp.bfloat16)
            store_scr[level * tiles + t] = solved.astype(jnp.bfloat16)
    own = solved_scr[:, :group, :]
    for other in range(1, cols // group):
        own = jnp.where(rep_ref[0] == other, solved_scr[:, other * group : (other + 1) * group, :], own)
    if last:
        for earlier in range(level):
            out_ref[earlier] = prev[earlier][...]
        out_ref[level] = own
        return
    out_ref[...] = own
    for earlier in range(level):
        for t in range(tiles):
            store_scr[earlier * tiles + t] = prev[earlier][t]
    for r in range(SLOTS):
        chosen_ref[r] = 0
    count = jnp.int32(0)
    for p in range(mats_ref.shape[1]):
        row = ids_ref[1, p] - HANDED * tiles
        live = jnp.logical_and(row >= 0, row < tiles)
        chosen_ref[jnp.minimum(count, SLOTS)] = jnp.int32(p)
        count = count + live.astype(jnp.int32)
    acc_scr[...] = jnp.zeros_like(acc_scr)
    for r in range(SLOTS):
        p = chosen_ref[r]
        update = jnp.dot(
            store_scr[ids_ref[0, p]], mats_ref[level, p], preferred_element_type=jnp.float32
        )
        row = jnp.where(r < count, ids_ref[1, p] - HANDED * tiles, tiles)
        acc_scr[row] = acc_scr[row] + update
    handed_ref[...] = acc_scr[:tiles].astype(jnp.bfloat16)


def panels_body(level, *refs):
    refs = list(refs)
    take = lambda count: [refs.pop(0) for _ in range(count)]
    ids_ref, mats_ref = take(2)
    stores = take(level + 1)
    own_ref, sibling_ref, far_ref, chip_ref, store_scr, updates_scr, acc_scr = refs
    tiles = own_ref.shape[0]
    for earlier in range(level + 1):
        for t in range(tiles):
            store_scr[earlier * tiles + t] = stores[earlier][t]
    for p in range(0, mats_ref.shape[1], 2):
        updates_scr[p], updates_scr[p + 1] = two_products(
            store_scr[ids_ref[0, p]],
            store_scr[ids_ref[0, p + 1]],
            mats_ref[level, p],
            mats_ref[level, p + 1],
        )
    acc_scr[...] = jnp.zeros_like(acc_scr)
    for p in range(mats_ref.shape[1]):
        slot = ids_ref[1, p]
        acc_scr[slot] = acc_scr[slot] + updates_scr[p]

    def sums(index):
        return acc_scr[index * tiles : (index + 1) * tiles].astype(jnp.bfloat16)

    own_ref[...] = sums(OWN)
    sibling_ref[...] = sums(SIBLING)
    far_ref[...] = sums(FAR)
    chip_ref[0] = sums(PASSED)
    chip_ref[1] = sums(DIRECT)


def last_body(*refs):
    *refs, out_ref = refs
    parts, diag_ref, earlier = refs[:4], refs[4], refs[5:]
    for level, ref in enumerate(earlier):
        out_ref[level] = ref[...]
    for t in range(diag_ref.shape[1]):
        residual = sum(part[t].astype(jnp.float32) for part in parts).astype(jnp.bfloat16)
        out_ref[len(earlier), t] = jnp.dot(residual, diag_ref[0, t], preferred_element_type=jnp.float32)


def run_last(parts, diag, results, shape):
    vmem = pl.BlockSpec(memory_space=pltpu.VMEM)
    args = [*parts, diag, *results]
    return pl.pallas_call(
        last_body,
        out_shape=jax.ShapeDtypeStruct(shape, jnp.float32),
        in_specs=[vmem] * len(args),
        out_specs=vmem,
        compiler_params=pltpu.CompilerParams(vmem_limit_bytes=6 << 20),
    )(*args)


def run_solve(level, last, rep, ids, parts, weights, prev, shape):
    levels, tiles, group, span = shape
    cols = 4 * group
    smem = pl.BlockSpec(memory_space=pltpu.SMEM)
    vmem = pl.BlockSpec(memory_space=pltpu.VMEM)
    scalars = [rep] if last else [rep, ids]
    inner = [*parts, *weights, *prev]
    scratch = [pltpu.VMEM((tiles, cols, span), jnp.float32)]
    if last:
        outs = jax.ShapeDtypeStruct(shape, jnp.float32)
        out_specs = vmem
    else:
        block = jax.ShapeDtypeStruct((tiles, cols, span), jnp.bfloat16)
        outs = [jax.ShapeDtypeStruct((tiles, group, span), jnp.float32), block, block]
        out_specs = [vmem] * len(outs)
        scratch.append(pltpu.VMEM(((level + 1) * tiles, cols, span), jnp.bfloat16))
        scratch.append(pltpu.VMEM((tiles + 1, cols, span), jnp.float32))
        scratch.append(pltpu.SMEM((SLOTS + 1,), jnp.int32))
    return pl.pallas_call(
        functools.partial(solve_body, level, last),
        out_shape=outs,
        in_specs=[smem] * len(scalars) + [vmem] * len(inner),
        out_specs=out_specs,
        scratch_shapes=scratch,
        compiler_params=pltpu.CompilerParams(vmem_limit_bytes=6 << 20),
    )(*scalars, *inner)


def run_panels(level, ids, mats, stores):
    smem = pl.BlockSpec(memory_space=pltpu.SMEM)
    vmem = pl.BlockSpec(memory_space=pltpu.VMEM)
    tiles, cols, span = stores[0].shape
    return pl.pallas_call(
        functools.partial(panels_body, level),
        out_shape=[
            jax.ShapeDtypeStruct((*lead, tiles, cols, span), jnp.bfloat16) for lead in ((), (), (), (2,))
        ],
        in_specs=[smem] + [vmem] * (1 + len(stores)),
        out_specs=[vmem] * 4,
        scratch_shapes=[
            pltpu.VMEM(((level + 1) * tiles, cols, span), jnp.bfloat16),
            pltpu.VMEM((mats.shape[1], cols, span), jnp.float32),
            pltpu.VMEM((GROUPS * tiles + 1, cols, span), jnp.float32),
        ],
        compiler_params=pltpu.CompilerParams(vmem_limit_bytes=6 << 20),
    )(ids, mats, *stores)


def slots_of(panel_dst, owner, dom_size, tiles):
    target = jnp.zeros_like(panel_dst)
    for other in range(1, dom_size):
        target = target + (panel_dst >= other * tiles).astype(jnp.int32)
    distance = target - owner
    distance = jnp.where(distance < 0, distance + dom_size, distance)
    near = jnp.where(distance > dom_size // 2, distance - dom_size, distance)
    onward = jnp.where(owner % 2 == 1, near, -near)
    group = jnp.where(
        distance == dom_size // 2,
        FAR,
        jnp.where(
            onward == 0,
            OWN,
            jnp.where(
                onward == 1, PASSED, jnp.where(onward == 2, DIRECT, jnp.where(onward == -1, SIBLING, HANDED))
            ),
        ),
    )
    return jnp.where(panel_dst >= 0, group * tiles + panel_dst - target * tiles, GROUPS * tiles)


def fetch_body(dom_size, *refs):
    owner_ref, _, src_hbm, dst_hbm, diag_hbm, mats_hbm, *ids_refs, diag_ref, mats_ref, src_ref, dst_ref, sems = refs
    lists = [
        pltpu.make_async_copy(src_hbm, src_ref, sems.at[1 + CHUNKS]),
        pltpu.make_async_copy(dst_hbm, dst_ref, sems.at[2 + CHUNKS]),
    ]
    for copy in lists:
        copy.start()
    copies = [pltpu.make_async_copy(diag_hbm.at[pl.ds(0, 1)], diag_ref, sems.at[0])]
    step = mats_ref.shape[1] // CHUNKS
    for chunk in range(CHUNKS):
        some = pl.ds(chunk * step, step)
        copies.append(
            pltpu.make_async_copy(mats_hbm.at[pl.ds(0, 1), some], mats_ref.at[:, some], sems.at[1 + chunk])
        )
    for copy in copies:
        copy.start()
    for copy in lists:
        copy.wait()
    slots = slots_of(dst_ref[...], owner_ref[0], dom_size, diag_ref.shape[1])
    for level, ids_ref in enumerate(ids_refs):
        ids_ref[0:1] = src_ref[level : level + 1]
        ids_ref[1:2] = slots[level : level + 1]
    for copy in copies:
        copy.wait()


def fetch(after, src, dst, diag, mats):
    vmem = pl.BlockSpec(memory_space=pltpu.VMEM)
    hbm = pl.BlockSpec(memory_space=pltpu.HBM)
    owner = lax.axis_index("dom").astype(jnp.int32)
    return pl.pallas_call(
        functools.partial(fetch_body, lax.axis_size("dom")),
        out_shape=[
            *[jax.ShapeDtypeStruct((2, src.shape[1]), jnp.int32) for _ in range(src.shape[0])],
            pltpu.VMEM((1, *diag.shape[1:]), diag.dtype),
            pltpu.VMEM((1, *mats.shape[1:]), mats.dtype),
        ],
        in_specs=[pl.BlockSpec(memory_space=pltpu.SMEM), vmem, hbm, hbm, hbm, hbm],
        out_specs=[vmem] * (2 + src.shape[0]),
        scratch_shapes=[pltpu.VMEM(src.shape, src.dtype), pltpu.VMEM(dst.shape, dst.dtype), pltpu.SemaphoreType.DMA((3 + CHUNKS,))],
        compiler_params=pltpu.CompilerParams(vmem_limit_bytes=1 << 20),
    )(owner[None], after, src, dst, diag, mats)


def next_diag_body(level, *refs):
    _, sibling_ref, diag_hbm, passed_ref, diag_ref, sems = refs
    tiles = diag_ref.shape[1]
    copies = [
        pltpu.make_async_copy(diag_hbm.at[pl.ds(level, 1), some], diag_ref.at[:, some], sems.at[half])
        for half, some in enumerate((pl.ds(0, tiles // 2), pl.ds(tiles // 2, tiles // 2)))
    ]
    for copy in copies:
        copy.start()
    passed_ref[...] = sibling_ref[...]
    for copy in copies:
        copy.wait()


def next_diag(level, after, sibling, diag):
    vmem = pl.BlockSpec(memory_space=pltpu.VMEM)
    return pl.pallas_call(
        functools.partial(next_diag_body, level),
        out_shape=[
            jax.ShapeDtypeStruct(sibling.shape, sibling.dtype),
            pltpu.VMEM((1, *diag.shape[1:]), diag.dtype),
        ],
        in_specs=[vmem, vmem, pl.BlockSpec(memory_space=pltpu.HBM)],
        out_specs=[vmem, vmem],
        scratch_shapes=[pltpu.SemaphoreType.DMA((2,))],
        compiler_params=pltpu.CompilerParams(vmem_limit_bytes=1 << 20),
    )(after, sibling, diag)


def per_device(right_sides, diag_inverse, panel_mats, panel_src, panel_dst):
    levels, tiles, group, span = right_sides.shape
    rep_size = lax.axis_size("rep")
    rep = lax.axis_index("rep").astype(jnp.int32)
    cols = group * rep_size
    top = lax.broadcasted_iota(jnp.int32, (2, tiles, cols, span), 0) == 0
    partial = right_sides[0].astype(jnp.bfloat16)
    place = lax.broadcasted_iota(jnp.int32, (levels, tiles, cols, span), 2) // group == rep
    own_rhs = jnp.where(place, jnp.concatenate([right_sides] * rep_size, 2), 0.0)
    src, dst, diag_hbm, mats_hbm = (
        pltpu.with_memory_space_constraint(x, pltpu.HBM)
        for x in (panel_src, panel_dst, diag_inverse, panel_mats)
    )
    *ids, diag, early_mats = fetch(partial, src, dst, diag_hbm, mats_hbm)
    late_mats = pltpu.with_memory_space_constraint(panel_mats, pltpu.VMEM)
    store = []
    results = []
    for level in range(levels):
        last = level + 1 == levels
        if last:
            pieces = [
                sum(
                    jnp.where(rep ^ apart == index, full[:, index * group : (index + 1) * group], 0.0)
                    for index in range(rep_size)
                ).astype(jnp.bfloat16)
                for apart in (0, *APART_FIRST)
            ]
            parts = pieces[:1] + [along_rep(piece, apart) for piece, apart in zip(pieces[1:], APART_FIRST)]
            return run_last(parts, diag, results, right_sides.shape)
        parts = [partial] + [
            along_rep(partial, apart) for apart in (APART if level else APART_FIRST)
        ]
        weights = [diag, late_mats if level else early_mats]
        solved, stored, handed = run_solve(
            level, last, rep[None], ids[level], parts, weights, store, right_sides.shape
        )
        results.append(solved)
        store.append(stored)
        own, sibling, far, chip = run_panels(level, ids[level], weights[1], store)
        handed = jnp.where(top, to_sibling(handed), jnp.zeros_like(handed))
        chip = (chip.astype(jnp.float32) + handed.astype(jnp.float32)).astype(jnp.bfloat16)
        from_chip = to_next_chip(chip)
        sibling, diag = next_diag(level + 1, chip, sibling, diag_hbm)
        from_far = to_far(far)
        across = to_sibling(
            (from_chip[1].astype(jnp.float32) + sibling.astype(jnp.float32)).astype(jnp.bfloat16)
        )
        incoming = sum(piece.astype(jnp.float32) for piece in (own, from_chip[0], from_far, across))
        full = own_rhs[level + 1] - incoming
        partial = full.astype(jnp.bfloat16)


def solution(mesh):
    return jax.shard_map(
        per_device,
        mesh=mesh,
        in_specs=(
            P(None, "dom", "rep", None),
            P(None, "dom", None, None),
            P(None, ("dom", "rep"), None, None),
            P(None, ("dom", "rep")),
            P(None, ("dom", "rep")),
        ),
        out_specs=P(None, "dom", "rep", None),
        check_vma=False,
    )
```
